32 devices in a mesh: groups: 2 (over x), seq: 16 (over z, y, core).
Axes of the slice: x: 2, y: 2, z: 4, core: 2. Of those that a mesh axis runs over, the one named last changes fastest.
Arguments:
- tokens: bfloat16 [32768, 1024], P(('groups', 'seq')), parts along dimension 0, may hold values from -6 to 6
- cotangent: bfloat16 [32768, 1024], P(('groups', 'seq')), parts along dimension 0, may hold values from -6 to 6
- gate_weight: bfloat16 [1024, 1024], P('seq'), may hold values from -0.1875 to 0.1875
- left_blocks: bfloat16 [32, 512, 512], P('seq'), may hold values from -0.25 to 0.25
- right_blocks: bfloat16 [512, 32, 32], P('seq'), may hold values from -1 to 1
Outputs:
- output: bfloat16 [32768, 1024], P(('groups', 'seq')), parts along dimension 0
- input_grad: bfloat16 [32768, 1024], P(('groups', 'seq')), parts along dimension 0
- gate_grad: float32 [2048, 1024], P(('groups', 'seq')), parts along dimension 0
- left_grad: bfloat16 [64, 512, 512], P(('groups', 'seq')), parts along dimension 0
- right_grad: bfloat16 [1024, 32, 32], P(('groups', 'seq')), parts along dimension 0
The draws below stay inside these ranges and needn't reach their ends.
There are 2 independent parts, one for each index of `groups`. The reference program is written for one: setup_inputs(seed, part) draws one part's arguments, and reference() takes and returns one part's arrays. A program takes and returns all parts, laid end to end along the dimension named above; an argument that names none is the same for every part. Nothing has to cross between parts.
All inputs are finite; a program needn't handle non-finite values.
Results may differ from the reference program's by a relative error of at most 0.0095.
Values may be sent and summed in bfloat16 or wider, within the bound.
A program may use at most 128 MiB of HBM per device.

```python
import jax
import jax.numpy as jnp

WIDTH = 1024
INNER = 512
OUTER = 32
TOKENS = 16384


def spiked(array, rng, source, target, blocks, factor):
    def block_of(dim):
        return (jnp.arange(array.shape[dim]) // (array.shape[dim] // blocks)).reshape((-1,) + (1,) * (array.ndim - 1 - dim))

    first = jax.random.permutation(rng, blocks)[block_of(target)]
    far = (block_of(target) + blocks // 2) % blocks
    return jnp.where((block_of(source) == first) | (block_of(source) == far), factor * array, array)


def block_scale(key, shape, cuts, least, high):
    loudness = 1.0
    for position, parts in cuts:
        steps = jax.random.uniform(jax.random.fold_in(jax.random.fold_in(key, 6), position), (parts,), jnp.float32, least / len(cuts), high / len(cuts))
        loudness = loudness * jnp.repeat(jnp.exp(steps), shape[position] // parts).reshape((-1,) + (1,) * (len(shape) - 1 - position))
    return loudness


def normal_values(own_key, shape, deviation, reach, split=(), kind=jnp.bfloat16):
    entries = deviation * jax.random.normal(own_key, shape, jnp.float32)
    if split:
        entries = entries * block_scale(own_key, shape, split, -0.22, 0.18)
    return jnp.clip(entries, -reach, reach).astype(kind)


def gaussian_with(stream_key, extent, scale, reach, pieces, heavy, held_as=jnp.bfloat16):
    drawn = scale * jax.random.normal(stream_key, extent, jnp.float32)
    if pieces:
        drawn = drawn * block_scale(stream_key, extent, pieces, -0.22, 0.18)
    return jnp.clip(spiked(drawn, jax.random.fold_in(stream_key, 3), *heavy), -reach, reach).astype(held_as)


def setup_inputs(seed: int = 0, part: int = 0) -> dict:
    key_of = jax.random.split(jax.random.key(seed), 6)
    part_keys = jax.random.split(jax.random.fold_in(key_of[5], part), 6)
    tokens = gaussian_with(part_keys[0], (TOKENS, WIDTH), 1.0, 6.0, ((0, 16),), (0, 1, 16, 2.0))
    cotangent = normal_values(part_keys[1], (TOKENS, WIDTH), 1.0, 6.0, ((0, 16),))
    gate_weight = normal_values(key_of[2], (WIDTH, WIDTH), WIDTH ** -0.5, 0.1875, ((0, 16),))
    left_blocks = normal_values(key_of[3], (OUTER, INNER, INNER), INNER ** -0.5, 0.25, ((0, 16),))
    right_blocks = normal_values(key_of[4], (INNER, OUTER, OUTER), OUTER ** -0.5, 1.0, ((0, 16),))
    return {"tokens": tokens, "cotangent": cotangent, "gate_weight": gate_weight, "left_blocks": left_blocks, "right_blocks": right_blocks}


def silu_slope(value):
    sig = jax.nn.sigmoid(value)
    return sig * (1.0 + value * (1.0 - sig))


def reference(tokens, cotangent, gate_weight, left_blocks, right_blocks):
    grid = tokens.reshape(OUTER, INNER, WIDTH).astype(jnp.float32)
    left_f = left_blocks.astype(jnp.float32)
    right_f = right_blocks.astype(jnp.float32)
    first = jnp.einsum('ajb,abc->ajc', left_f, grid).astype(jnp.bfloat16)
    second = jnp.einsum('bia,abc->ibc', right_f, first.astype(jnp.float32)).astype(jnp.bfloat16)
    gate = jnp.dot(tokens, gate_weight, preferred_element_type=jnp.float32).astype(jnp.bfloat16)
    gate_f = gate.reshape(OUTER, INNER, WIDTH).astype(jnp.float32)
    factor = jax.nn.silu(gate_f)
    second_f = second.astype(jnp.float32)
    output = (second_f * factor).astype(jnp.bfloat16)
    upstream = cotangent.reshape(OUTER, INNER, WIDTH).astype(jnp.float32)
    second_grad = (upstream * factor).astype(jnp.bfloat16)
    gate_delta = (upstream * second_f * silu_slope(gate_f)).astype(jnp.bfloat16)
    second_grad_f = second_grad.astype(jnp.float32)
    first_grad = jnp.einsum('bia,ibc->abc', right_f, second_grad_f).astype(jnp.bfloat16)
    scale_w = WIDTH ** -0.5
    right_grad = (jnp.einsum('ibc,abc->bia', second_grad_f, first.astype(jnp.float32)) * scale_w).astype(jnp.bfloat16)
    first_grad_f = first_grad.astype(jnp.float32)
    left_grad = (jnp.einsum('ajc,abc->ajb', first_grad_f, grid) * scale_w).astype(jnp.bfloat16)
    mixer_part = jnp.einsum('ajb,ajc->abc', left_f, first_grad_f).reshape(TOKENS, WIDTH)
    delta_flat = gate_delta.reshape(TOKENS, WIDTH)
    gate_part = jnp.dot(delta_flat, gate_weight.T, preferred_element_type=jnp.float32)
    input_grad = (mixer_part + gate_part).astype(jnp.bfloat16)
    gate_grad = jnp.dot(tokens.T, delta_flat, preferred_element_type=jnp.float32) * (TOKENS ** -0.5)
    return (output.reshape(TOKENS, WIDTH), input_grad, gate_grad, left_grad, right_grad)
```

```python
import functools

import jax
import jax.numpy as jnp
from jax import lax
from jax.experimental import pallas as pl
from jax.experimental.pallas import tpu as pltpu
from jax.sharding import PartitionSpec as P


def silu_slope(value):
    sig = jax.nn.sigmoid(value)
    return sig * (1.0 + value * (1.0 - sig))


def to_columns(values):
    return lax.all_to_all(values, "seq", split_axis=1, concat_axis=0, tiled=True)


def to_rows(values):
    return lax.all_to_all(values, "seq", split_axis=0, concat_axis=1, tiled=True)


def body(tokens, cotangent, gate_weight, left_blocks, right_blocks):
    seq_count = lax.axis_size("seq")
    local_blocks = left_blocks.shape[0]
    block_size = left_blocks.shape[1]
    tok_rows = tokens.shape[0]
    channels = tokens.shape[1]
    token_grid = tokens.reshape(local_blocks, block_size, channels)
    upstream = cotangent.reshape(local_blocks, block_size, channels)
    first = jnp.einsum(
        "ajb,abc->ajc", left_blocks, token_grid, preferred_element_type=jnp.float32
    ).astype(jnp.bfloat16)
    full_weight = lax.all_gather(gate_weight, "seq", axis=0, tiled=True)
    gate_sum = jnp.dot(tokens, full_weight, preferred_element_type=jnp.float32)
    gate = gate_sum.astype(jnp.bfloat16).reshape(local_blocks, block_size, channels)
    first_cols = to_columns(first)
    second_cols = jnp.einsum(
        "bia,abc->ibc", right_blocks, first_cols, preferred_element_type=jnp.float32
    ).astype(jnp.bfloat16)
    second = to_rows(second_cols)
    gate_f = gate.astype(jnp.float32)
    factor = jax.nn.silu(gate_f)
    second_f = second.astype(jnp.float32)
    upstream_f = upstream.astype(jnp.float32)
    output = (second_f * factor).astype(jnp.bfloat16)
    second_grad = (upstream_f * factor).astype(jnp.bfloat16)
    gate_delta = (upstream_f * second_f * silu_slope(gate_f)).astype(jnp.bfloat16)
    grad_cols = to_columns(second_grad)
    first_grad_cols = jnp.einsum(
        "bia,ibc->abc", right_blocks, grad_cols, preferred_element_type=jnp.float32
    ).astype(jnp.bfloat16)
    scale_w = channels ** (-0.5)
    right_grad = (
        jnp.einsum("ibc,abc->bia", grad_cols, first_cols, preferred_element_type=jnp.float32)
        * scale_w
    ).astype(jnp.bfloat16)
    first_grad = to_rows(first_grad_cols)
    left_grad = (
        jnp.einsum("ajc,abc->ajb", first_grad, token_grid, preferred_element_type=jnp.float32)
        * scale_w
    ).astype(jnp.bfloat16)
    mixer_part = jnp.einsum(
        "ajb,ajc->abc", left_blocks, first_grad, preferred_element_type=jnp.float32
    ).reshape(tok_rows, channels)
    delta_flat = gate_delta.reshape(tok_rows, channels)
    gate_part = jnp.einsum("tc,kc->tk", delta_flat, full_weight, preferred_element_type=jnp.float32)
    input_grad = (mixer_part + gate_part).astype(jnp.bfloat16)
    weight_term = jnp.einsum("tk,tc->kc", tokens, delta_flat, preferred_element_type=jnp.float32)
    gate_grad = lax.psum_scatter(weight_term, "seq", scatter_dimension=0, tiled=True)
    gate_grad = gate_grad * (tok_rows * seq_count) ** (-0.5)
    return (output.reshape(tok_rows, channels), input_grad, gate_grad, left_grad, right_grad)


F32 = jnp.float32
BF16 = jnp.bfloat16
ROWS = 16
PLANE = 4


def mixer_kernel(
    n, tok_hbm, cot_hbm, wsh, left_hbm, right_hbm,
    tok, left, out, part, fr, lgrad, ggrad, rgrad,
    right, cot, wf, first_s, sg_s, fc, gc, sc, fgc, sr, gate, delta, wt, half, quarter, pair, tail, mix,
    ssem, rsem, ws_sem, wr_sem, gs_sem, gr_sem, lsem,
):
    me = lax.axis_index("seq")
    zi, qi = me // PLANE, me % PLANE
    chunks = fc.shape[0]
    blocks, width = tok.shape[0], tok.shape[2]
    nz = n // PLANE
    deep = fc.shape[1] * ROWS
    tile = 256
    per = tile // ROWS
    row_tiles = tok.shape[1] // tile
    owners = per // chunks

    loads = [
        pltpu.make_async_copy(left_hbm, left, lsem.at[0]),
        pltpu.make_async_copy(tok_hbm, tok, lsem.at[1]),
        pltpu.make_async_copy(wsh, wf.at[zi, qi], lsem.at[2]),
        pltpu.make_async_copy(cot_hbm, cot, lsem.at[3]),
        pltpu.make_async_copy(right_hbm, right, lsem.at[4]),
    ]

    barrier = pltpu.get_barrier_semaphore()

    def greet(s, carry):
        pl.semaphore_signal(barrier, inc=1, device_id={"seq": (me + s) % n}, device_id_type=pl.DeviceIdType.MESH)
        return carry

    lax.fori_loop(1, n, greet, 0)
    for load in loads:
        load.start()
    loads[0].wait()
    loads[1].wait()

    def first_tile(t, carry):
        a, j = t // row_tiles, t % row_tiles
        side = left[a, pl.ds(j * owners, owners)].reshape(tile, left.shape[4])
        prod = jnp.dot(side, tok[a], preferred_element_type=F32)
        first_s[a, pl.ds(j * per, per)] = prod.astype(BF16).reshape(per, ROWS, width)
        return carry

    lax.fori_loop(0, blocks * row_tiles, first_tile, 0)
    pl.semaphore_wait(barrier, n - 1)

    def remote(src, dst, ss, rs, dev):
        return pltpu.make_async_remote_copy(
            src_ref=src, dst_ref=dst, send_sem=ss, recv_sem=rs,
            device_id={"seq": dev}, device_id_type=pl.DeviceIdType.MESH,
        )

    def to_cols(ph, k, src, dst, s):
        t = (s * 7) % n
        peer = (me + t) % n
        return remote(
            src.at[:, peer * chunks + k], dst.at[k, pl.ds(me * blocks, blocks)],
            ssem.at[ph, k, t], rsem.at[ph, k, t], peer,
        )

    def to_rows_(ph, k, src, dst, s):
        t = (s * 7) % n
        peer = (me + t) % n
        return remote(
            src.at[k, pl.ds(peer * blocks, blocks)], dst.at[:, k, me],
            ssem.at[ph, k, t], rsem.at[ph, k, t], peer,
        )

    def each(make, action):
        def step(s, carry):
            copy = make(s)
            if action == "start":
                copy.start()
            elif action == "recv":
                copy.wait_recv()
            else:
                copy.wait_send()
            return carry

        lax.fori_loop(1, n, step, 0)

    across = (zi + nz // 2) % nz
    beside = zi + 1 - 2 * (zi % 2)

    w_far = remote(wsh, wf.at[zi, qi], ws_sem.at[0, 0], wr_sem.at[0, 0], across * PLANE + qi)
    w_near = remote(wsh, wf.at[zi, qi], ws_sem.at[0, 1], wr_sem.at[0, 1], beside * PLANE + qi)
    w_pass = remote(wf.at[across, qi], wf.at[across, qi], ws_sem.at[0, 2], wr_sem.at[0, 2], beside * PLANE + qi)

    def w_q(d):
        return remote(wf.at[:, qi], wf.at[:, qi], ws_sem.at[1, d], wr_sem.at[1, d], zi * PLANE + (qi + d) % PLANE)

    w_far.start()
    w_near.start()

    def send_first(k):
        each(functools.partial(to_cols, 0, k, first_s, fc), "start")
        fc[k, pl.ds(me * blocks, blocks)] = first_s[:, me * chunks + k]

    def send_second_grad(k):
        each(functools.partial(to_cols, 1, k, sg_s, gc), "start")
        gc[k, pl.ds(me * blocks, blocks)] = sg_s[:, me * chunks + k]

    send_first(0)
    w_far.wait_recv()
    w_pass.start()
    for k in range(1, chunks):
        send_first(k)

    spread = (
        lax.broadcasted_iota(jnp.int32, (deep // ROWS, deep), 1) // ROWS
        == lax.broadcasted_iota(jnp.int32, (deep // ROWS, deep), 0)
    ).astype(F32).astype(BF16)
    same = (
        lax.broadcasted_iota(jnp.int32, (deep, deep), 0) % ROWS
        == lax.broadcasted_iota(jnp.int32, (deep, deep), 1) % ROWS
    )
    outer = deep // ROWS
    row = lax.broadcasted_iota(jnp.int32, (deep, deep), 0)
    col = lax.broadcasted_iota(jnp.int32, (deep, deep), 1)
    turn = ((row // ROWS == col % outer) & (row % ROWS == col // outer)).astype(F32).astype(BF16)
    loads[4].wait()
    for k in range(chunks):
        rk = jnp.dot(turn, right[k], preferred_element_type=F32).astype(BF16)
        wide = jnp.dot(rk, spread, preferred_element_type=F32)
        mix[k] = jnp.where(same, wide, 0.0).astype(BF16)

    def mixed(k, src, dst, dims):
        def step(t, carry):
            cols = pl.ds(pl.multiple_of(t * tile, tile), tile)
            x = src[k, :, :, cols].reshape(deep, tile)
            y = lax.dot_general(mix[k], x, (dims, ((), ())), preferred_element_type=F32)
            dst[k, :, :, cols] = y.astype(BF16).reshape(deep // ROWS, ROWS, tile)
            return carry

        lax.fori_loop(0, width // tile, step, 0)

    def second_of(k):
        each(functools.partial(to_cols, 0, k, first_s, fc), "recv")
        mixed(k, fc, sc, ((1,), (0,)))
        each(functools.partial(to_rows_, 2, k, sc, sr), "start")
        sr[:, k, me] = sc[k, pl.ds(me * blocks, blocks)]

    def first_grad_of(k):
        each(functools.partial(to_cols, 1, k, sg_s, gc), "recv")
        mixed(k, gc, fgc, ((0,), (0,)))
        each(functools.partial(to_rows_, 3, k, fgc, fr), "start")
        fr[:, k, me] = fgc[k, pl.ds(me * blocks, blocks)]

    second_of(0)
    loads[2].wait()
    w_near.wait_recv()
    w_pass.wait_recv()
    for d in range(1, PLANE):
        w_q(d).start()
    for k in range(1, chunks):
        second_of(k)

    for d in range(1, PLANE):
        w_q(d).wait_recv()
    loads[3].wait()

    def gate_tile(t, carry):
        a, j = t // row_tiles, t % row_tiles
        rows = pl.ds(j * tile, tile)
        weight = wf[...].reshape(width, width)
        g = jnp.dot(tok[a, rows, :], weight, preferred_element_type=F32).astype(BF16)
        gate[a, rows, :] = g
        gf = g.astype(F32)
        up = cot[a, rows, :].astype(F32) * (gf * jax.nn.sigmoid(gf))
        sg_s[a, pl.ds(j * per, per)] = up.astype(BF16).reshape(per, ROWS, width)
        return carry

    lax.fori_loop(0, blocks * row_tiles, gate_tile, 0)
    send_second_grad(0)

    for k in range(chunks):
        each(functools.partial(to_rows_, 2, k, sc, sr), "recv")

    def delta_tile(t, carry):
        a, j = t // row_tiles, t % row_tiles
        rows = pl.ds(j * tile, tile)
        gf = gate[a, rows, :].astype(F32)
        sig = jax.nn.sigmoid(gf)
        sec = jnp.stack([sr[a, k, pl.ds(j * owners, owners)] for k in range(chunks)], axis=1)
        sec = sec.reshape(tile, width).astype(F32)
        up = cot[a, rows, :].astype(F32)
        out[a, rows, :] = (sec * (gf * sig)).astype(BF16)
        delta[a, rows, :] = (up * sec * (sig * (1.0 + gf * (1.0 - sig)))).astype(BF16)
        return carry

    lax.fori_loop(0, blocks * row_tiles, delta_tile, 0)
    def weight_tile(z, carry):
        cols = pl.ds(pl.multiple_of(z * tile, tile), tile)
        tokens_2d = tok[:, :, cols].reshape(blocks * tok.shape[1], tile)
        delta_2d = delta[...].reshape(blocks * tok.shape[1], width)
        prod = lax.dot_general(tokens_2d, delta_2d, (((0,), (0,)), ((), ())), preferred_element_type=F32)
        wt[z] = prod.astype(BF16).reshape(PLANE, tile // PLANE, width)
        return carry

    lax.fori_loop(0, width // tile, weight_tile, 0)

    def g_q(d):
        peer = (qi + d) % PLANE
        return remote(wt.at[:, peer], half.at[d - 1], gs_sem.at[0, d], gr_sem.at[0, d], zi * PLANE + peer)

    g_near = [
        remote(quarter.at[beside], tail.at[0], gs_sem.at[1, 0], gr_sem.at[1, 0], beside * PLANE + qi),
        remote(
            quarter.at[(beside + nz // 2) % nz], tail.at[1], gs_sem.at[1, 1], gr_sem.at[1, 1], beside * PLANE + qi
        ),
    ]
    g_far = remote(pair, tail.at[2], gs_sem.at[1, 2], gr_sem.at[1, 2], across * PLANE + qi)

    for d in range(1, PLANE):
        g_q(d).start()

    for k in range(1, chunks):
        send_second_grad(k)

    for d in range(1, PLANE):
        g_q(d).wait_recv()

    def sum_tile(z, carry):
        total = wt[z, qi].astype(F32)
        for d in range(PLANE - 1):
            total = total + half[d, z].astype(F32)
        quarter[z] = total.astype(BF16)
        return carry

    lax.fori_loop(0, nz, sum_tile, 0)
    for copy in g_near:
        copy.start()
    first_grad_of(0)

    for copy in g_near:
        copy.wait_recv()
    pair[...] = (quarter[across].astype(F32) + tail[1].astype(F32)).astype(BF16)
    g_far.start()
    for k in range(1, chunks):
        first_grad_of(k)

    def part_tile(t, carry):
        a, j = t // row_tiles, t % row_tiles
        rows = pl.ds(j * tile, tile)
        weight = wf[...].reshape(width, width)
        part[a, rows, :] = lax.dot_general(
            delta[a, rows, :], weight, (((1,), (1,)), ((), ())), preferred_element_type=F32
        )
        return carry

    lax.fori_loop(0, blocks * row_tiles, part_tile, 0)

    scale_w = width ** (-0.5)
    for k in range(chunks):
        pairs = lax.dot_general(
            gc[k].reshape(deep, width), fc[k].reshape(deep, width),
            (((1,), (1,)), ((), ())), preferred_element_type=F32,
        )
        kept = jnp.where(same, pairs * scale_w, 0.0).astype(BF16)
        picked = lax.dot_general(
            kept, spread, (((1,), (1,)), ((), ())), preferred_element_type=F32
        ).astype(BF16)
        rgrad[k] = lax.dot_general(
            turn, picked, (((0,), (0,)), ((), ())), preferred_element_type=F32
        ).astype(BF16)

    g_far.wait_recv()
    total = quarter[zi].astype(F32) + tail[0].astype(F32) + tail[2].astype(F32)
    ggrad[...] = total * (blocks * tok.shape[1] * n) ** (-0.5)

    for k in range(chunks):
        each(functools.partial(to_cols, 0, k, first_s, fc), "send")
        each(functools.partial(to_rows_, 2, k, sc, sr), "send")
        each(functools.partial(to_cols, 1, k, sg_s, gc), "send")
    for copy in (w_far, w_near, w_pass, *g_near, g_far):
        copy.wait_send()
    for d in range(1, PLANE):
        w_q(d).wait_send()
        g_q(d).wait_send()

    for k in range(chunks - 1):
        each(functools.partial(to_rows_, 3, k, fgc, fr), "recv")
        each(functools.partial(to_rows_, 3, k, fgc, fr), "send")

        def near_tile(t, carry):
            a, j = t // row_tiles, t % row_tiles
            rows = pl.ds(pl.multiple_of(j * tile, tile), tile)
            part[a, rows, :] += mixer_of(a, k, rows, left, fr)
            lgrad[a, k, :, :, rows] = left_grad_of(a, k, rows, tok, fr)
            return carry

        lax.fori_loop(0, blocks * row_tiles, near_tile, 0)

    for k in range(chunks - 1, chunks):
        each(functools.partial(to_rows_, 3, k, fgc, fr), "send")
        each(functools.partial(to_rows_, 3, k, fgc, fr), "recv")


def mixer_of(a, k, rows, left, fr):
    high = fr.shape[2] * ROWS
    side = left[a, :, k, :, rows].reshape(high, rows.size)
    grad = fr[a, k].reshape(high, fr.shape[4])
    return lax.dot_general(side, grad, (((0,), (0,)), ((), ())), preferred_element_type=F32)


def left_grad_of(a, k, rows, tok, fr):
    high, width = fr.shape[2] * ROWS, fr.shape[4]
    grad = fr[a, k].reshape(high, width)
    lg = lax.dot_general(grad, tok[a, rows, :], (((1,), (1,)), ((), ())), preferred_element_type=F32)
    return (lg * width ** (-0.5)).astype(BF16).reshape(fr.shape[2], ROWS, rows.size)


def last_kernel(
    tok, left, out_in, part, fr, lgrad_in, ggrad_in, rgrad_in,
    out, igrad, lgrad, ggrad, rgrad,
    ig, lg, sem, ig_sem,
):
    blocks, chunks = fr.shape[0], fr.shape[1]
    tile = 256
    last = chunks - 1
    copies = [
        pltpu.make_async_copy(out_in, out, sem.at[0]),
        pltpu.make_async_copy(ggrad_in, ggrad, sem.at[1]),
        pltpu.make_async_copy(rgrad_in, rgrad, sem.at[2]),
    ]
    for k in range(last):
        copies.append(pltpu.make_async_copy(lgrad_in.at[:, k], lgrad.at[:, :, k], sem.at[4 + k]))
    for copy in copies:
        copy.start()
    for a in range(blocks):
        for j in range(tok.shape[1] // tile):
            rows = pl.ds(j * tile, tile)
            lg[a, :, :, rows] = left_grad_of(a, last, rows, tok, fr)
            ig[a, rows, :] = (part[a, rows, :] + mixer_of(a, last, rows, left, fr)).astype(BF16)
            copy = pltpu.make_async_copy(ig.at[a, rows], igrad.at[a, rows], ig_sem.at[a, j])
            copy.start()
            copies.append(copy)
    copy = pltpu.make_async_copy(lg, lgrad.at[:, :, last], sem.at[3])
    copy.start()
    for copy in (*copies, copy):
        copy.wait()


def fused_body(n, tokens, cotangent, gate_weight, left_blocks, right_blocks):
    blocks, inner = left_blocks.shape[0], left_blocks.shape[1]
    own, outer = right_blocks.shape[0], right_blocks.shape[1]
    width = tokens.shape[1]
    chunks = own // ROWS
    groups = inner // ROWS
    deep = outer * ROWS
    nz = n // PLANE
    shard = width // n
    rows = (blocks, inner, width)
    split = (blocks, n, chunks, ROWS, inner)
    near = (blocks, chunks - 1, n, ROWS, inner)
    by_row = pltpu.VMEM((blocks, groups, ROWS, width), BF16)
    by_owner = (blocks, chunks, n, ROWS, width)
    by_col = pltpu.VMEM((chunks, outer, ROWS, width), BF16)
    vmem = pl.BlockSpec(memory_space=pltpu.VMEM)
    hbm = pl.BlockSpec(memory_space=pltpu.HBM)
    args = (
        tokens.reshape(rows), cotangent.reshape(rows), gate_weight, left_blocks.reshape(split),
        right_blocks.reshape(chunks, deep, outer),
    )
    kept = pl.pallas_call(
        functools.partial(mixer_kernel, n),
        out_shape=(
            pltpu.VMEM(rows, BF16),
            pltpu.VMEM(split, BF16),
            pltpu.VMEM(rows, BF16),
            pltpu.VMEM(rows, F32),
            pltpu.VMEM(by_owner, BF16),
            pltpu.VMEM(near, BF16),
            pltpu.VMEM((shard, width), F32),
            pltpu.VMEM((chunks, deep, outer), BF16),
        ),
        in_specs=[hbm] * 5,
        out_specs=[vmem] * 8,
        scratch_shapes=[
            pltpu.VMEM((chunks, deep, outer), BF16),
            pltpu.VMEM(rows, BF16),
            pltpu.VMEM((nz, PLANE, shard, width), BF16),
            by_row, by_row, by_col, by_col, by_col, by_col, pltpu.VMEM(by_owner, BF16),
            pltpu.VMEM(rows, BF16),
            pltpu.VMEM(rows, BF16),
            pltpu.VMEM((nz, PLANE, shard, width), BF16),
            pltpu.VMEM((PLANE - 1, nz, shard, width), BF16),
            pltpu.VMEM((nz, shard, width), BF16),
            pltpu.VMEM((shard, width), BF16),
            pltpu.VMEM((3, shard, width), BF16),
            pltpu.VMEM((chunks, deep, deep), BF16),
            pltpu.SemaphoreType.DMA((4, chunks, n)),
            pltpu.SemaphoreType.DMA((4, chunks, n)),
            pltpu.SemaphoreType.DMA((2, PLANE)),
            pltpu.SemaphoreType.DMA((2, PLANE)),
            pltpu.SemaphoreType.DMA((2, PLANE)),
            pltpu.SemaphoreType.DMA((2, PLANE)),
            pltpu.SemaphoreType.DMA((5,)),
        ],
        compiler_params=pltpu.CompilerParams(
            collective_id=0, has_side_effects=True, vmem_limit_bytes=36 * 2**20
        ),
    )(*[pltpu.with_memory_space_constraint(x, pltpu.HBM) for x in args])
    out, igrad, lgrad, ggrad, rgrad = pl.pallas_call(
        last_kernel,
        out_shape=(
            jax.ShapeDtypeStruct(rows, BF16),
            jax.ShapeDtypeStruct(rows, BF16),
            jax.ShapeDtypeStruct(split, BF16),
            jax.ShapeDtypeStruct((shard, width), F32),
            jax.ShapeDtypeStruct((chunks, deep, outer), BF16),
        ),
        in_specs=[vmem] * 8,
        out_specs=[hbm] * 5,
        scratch_shapes=[
            pltpu.VMEM(rows, BF16),
            pltpu.VMEM((blocks, n, ROWS, inner), BF16),
            pltpu.SemaphoreType.DMA((3 + chunks,)),
            pltpu.SemaphoreType.DMA((blocks, inner // 256)),
        ],
        compiler_params=pltpu.CompilerParams(vmem_limit_bytes=12 * 2**20),
    )(*[pltpu.with_memory_space_constraint(x, pltpu.VMEM) for x in kept])
    return (
        out.reshape(tokens.shape), igrad.reshape(tokens.shape), ggrad, lgrad.reshape(left_blocks.shape),
        rgrad.reshape(own, outer, outer),
    )


def chosen_body(tokens, cotangent, gate_weight, left_blocks, right_blocks):
    n = lax.axis_size("seq")
    own, width, inner = right_blocks.shape[0], tokens.shape[1], left_blocks.shape[1]
    if n == PLANE * PLANE and own % ROWS == 0 and width == 256 * PLANE and inner % 256 == 0:
        return fused_body(n, tokens, cotangent, gate_weight, left_blocks, right_blocks)
    return body(tokens, cotangent, gate_weight, left_blocks, right_blocks)


def solution(mesh):
    in_specs = (
        P(("groups", "seq"), None),
        P(("groups", "seq"), None),
        P("seq", None),
        P("seq", None, None),
        P("seq", None, None),
    )
    out_specs = (
        P(("groups", "seq"), None),
        P(("groups", "seq"), None),
        P(("groups", "seq"), None),
        P(("groups", "seq"), None, None),
        P(("groups", "seq"), None, None),
    )
    return jax.shard_map(chosen_body, mesh=mesh, in_specs=in_specs, out_specs=out_specs, check_vma=False)
```

```python
import functools

import jax
import jax.numpy as jnp
from jax import lax
from jax.experimental import pallas as pl
from jax.experimental.pallas import tpu as pltpu
from jax.sharding import PartitionSpec as P


def silu_slope(value):
    sig = jax.nn.sigmoid(value)
    return sig * (1.0 + value * (1.0 - sig))


def to_columns(values):
    return lax.all_to_all(values, "seq", split_axis=1, concat_axis=0, tiled=True)


def to_rows(values):
    return lax.all_to_all(values, "seq", split_axis=0, concat_axis=1, tiled=True)


def body(tokens, cotangent, gate_weight, left_blocks, right_blocks):
    seq_count = lax.axis_size("seq")
    local_blocks = left_blocks.shape[0]
    block_size = left_blocks.shape[1]
    tok_rows = tokens.shape[0]
    channels = tokens.shape[1]
    token_grid = tokens.reshape(local_blocks, block_size, channels)
    upstream = cotangent.reshape(local_blocks, block_size, channels)
    first = jnp.einsum(
        "ajb,abc->ajc", left_blocks, token_grid, preferred_element_type=jnp.float32
    ).astype(jnp.bfloat16)
    full_weight = lax.all_gather(gate_weight, "seq", axis=0, tiled=True)
    gate_sum = jnp.dot(tokens, full_weight, preferred_element_type=jnp.float32)
    gate = gate_sum.astype(jnp.bfloat16).reshape(local_blocks, block_size, channels)
    first_cols = to_columns(first)
    second_cols = jnp.einsum(
        "bia,abc->ibc", right_blocks, first_cols, preferred_element_type=jnp.float32
    ).astype(jnp.bfloat16)
    second = to_rows(second_cols)
    gate_f = gate.astype(jnp.float32)
    factor = jax.nn.silu(gate_f)
    second_f = second.astype(jnp.float32)
    upstream_f = upstream.astype(jnp.float32)
    output = (second_f * factor).astype(jnp.bfloat16)
    second_grad = (upstream_f * factor).astype(jnp.bfloat16)
    gate_delta = (upstream_f * second_f * silu_slope(gate_f)).astype(jnp.bfloat16)
    grad_cols = to_columns(second_grad)
    first_grad_cols = jnp.einsum(
        "bia,ibc->abc", right_blocks, grad_cols, preferred_element_type=jnp.float32
    ).astype(jnp.bfloat16)
    scale_w = channels ** (-0.5)
    right_grad = (
        jnp.einsum("ibc,abc->bia", grad_cols, first_cols, preferred_element_type=jnp.float32)
        * scale_w
    ).astype(jnp.bfloat16)
    first_grad = to_rows(first_grad_cols)
    left_grad = (
        jnp.einsum("ajc,abc->ajb", first_grad, token_grid, preferred_element_type=jnp.float32)
        * scale_w
    ).astype(jnp.bfloat16)
    mixer_part = jnp.einsum(
        "ajb,ajc->abc", left_blocks, first_grad, preferred_element_type=jnp.float32
    ).reshape(tok_rows, channels)
    delta_flat = gate_delta.reshape(tok_rows, channels)
    gate_part = jnp.einsum("tc,kc->tk", delta_flat, full_weight, preferred_element_type=jnp.float32)
    input_grad = (mixer_part + gate_part).astype(jnp.bfloat16)
    weight_term = jnp.einsum("tk,tc->kc", tokens, delta_flat, preferred_element_type=jnp.float32)
    gate_grad = lax.psum_scatter(weight_term, "seq", scatter_dimension=0, tiled=True)
    gate_grad = gate_grad * (tok_rows * seq_count) ** (-0.5)
    return (output.reshape(tok_rows, channels), input_grad, gate_grad, left_grad, right_grad)


F32 = jnp.float32
BF16 = jnp.bfloat16
ROWS = 16
PLANE = 4


def mixer_kernel(
    n, tok_hbm, cot_hbm, wsh, left_hbm, right_hbm,
    tok, left, out, part, fr, lgrad, ggrad, rgrad,
    right, cot, wf, first_s, sg_s, fc, gc, sc, fgc, sr, gate, delta, wt, half, quarter, pair, tail, mix,
    ssem, rsem, ws_sem, wr_sem, gs_sem, gr_sem, lsem, step_sem,
):
    me = lax.axis_index("seq")
    zi, qi = me // PLANE, me % PLANE
    chunks = fc.shape[0]
    blocks, width = tok.shape[0], tok.shape[2]
    nz = n // PLANE
    deep = fc.shape[1] * ROWS
    tile = 256
    per = tile // ROWS
    row_tiles = tok.shape[1] // tile
    owners = per // chunks

    loads = [
        pltpu.make_async_copy(left_hbm, left, lsem.at[0]),
        pltpu.make_async_copy(tok_hbm, tok, lsem.at[1]),
        pltpu.make_async_copy(wsh, wf.at[zi, qi], lsem.at[2]),
        pltpu.make_async_copy(cot_hbm, cot, lsem.at[3]),
        pltpu.make_async_copy(right_hbm, right, lsem.at[4]),
    ]

    gi = lax.axis_index("groups")
    yi, ci = qi // 2, qi % 2
    middle = ((zi + 1) // 2) % 2
    adjacent = 5 + 2 * middle
    facing = nz - 1 - zi

    def tell(sem):
        def signal(dev):
            pl.semaphore_signal(sem, inc=1, device_id={"seq": dev}, device_id_type=pl.DeviceIdType.MESH)

        signal(me + 1 - 2 * ci)
        for c in range(2):
            signal(zi * PLANE + (1 - yi) * 2 + c)
            pl.when(zi > 0)(functools.partial(signal, (zi - 1) * PLANE + yi * 2 + c))
            pl.when(zi < nz - 1)(functools.partial(signal, (zi + 1) * PLANE + yi * 2 + c))

    barrier = pltpu.get_barrier_semaphore()
    pl.semaphore_signal(barrier, inc=1, device_id={"groups": 1 - gi}, device_id_type=pl.DeviceIdType.MESH)
    tell(barrier)
    for load in loads:
        load.start()
    pl.semaphore_wait(barrier, adjacent + 1)

    def remote(src, dst, ss, rs, dev):
        return pltpu.make_async_remote_copy(
            src_ref=src, dst_ref=dst, send_sem=ss, recv_sem=rs,
            device_id={"seq": dev}, device_id_type=pl.DeviceIdType.MESH,
        )

    def to_cols(ph, k, src, dst, s):
        t = (s * 7) % n
        peer = (me + t) % n
        return remote(
            src.at[:, peer * chunks + k], dst.at[k, pl.ds(me * blocks, blocks)],
            ssem.at[ph, k, t], rsem.at[ph, k, t], peer,
        )

    def to_rows_(ph, k, src, dst, s):
        t = (s * 7) % n
        peer = (me + t) % n
        return remote(
            src.at[k, pl.ds(peer * blocks, blocks)], dst.at[:, k, me],
            ssem.at[ph, k, t], rsem.at[ph, k, t], peer,
        )

    def each(make, action):
        def step(s, carry):
            copy = make(s)
            if action == "start":
                copy.start()
            elif action == "recv":
                copy.wait_recv()
            else:
                copy.wait_send()
            return carry

        lax.fori_loop(1, n, step, 0)

    across = (zi + nz // 2) % nz
    beside = zi + 1 - 2 * (zi % 2)
    own_first = (ci + gi + 1) % 2
    carried = facing * own_first + across * (1 - own_first)
    other_half = pl.ds((1 - zi // 2) * 2, 2)

    w_near = remote(wsh, wf.at[zi, qi], ws_sem.at[0, 1], wr_sem.at[0, 1], beside * PLANE + qi)
    w_own = remote(wsh, wf.at[zi, qi], ws_sem.at[0, 0], wr_sem.at[0, 0], facing * PLANE + qi)
    w_next = remote(wf.at[beside, qi], wf.at[beside, qi], ws_sem.at[0, 0], wr_sem.at[0, 0], facing * PLANE + qi)
    w_got = remote(wf.at[carried, qi], wf.at[carried, qi], ws_sem.at[0, 0], wr_sem.at[0, 0], facing * PLANE + qi)
    w_group = pltpu.make_async_remote_copy(
        src_ref=wf.at[carried, qi], dst_ref=wf.at[carried, qi], send_sem=ws_sem.at[0, 3], recv_sem=wr_sem.at[0, 3],
        device_id={"groups": 1 - gi}, device_id_type=pl.DeviceIdType.MESH,
    )
    w_pass = remote(
        wf.at[other_half, qi], wf.at[other_half, qi], ws_sem.at[0, 2], wr_sem.at[0, 2], beside * PLANE + qi
    )

    mate = me + 1 - 2 * ci
    over = (1 - yi) * 2 + ci
    w_y = remote(wf.at[:, qi], wf.at[:, qi], ws_sem.at[1, 0], wr_sem.at[1, 0], zi * PLANE + over)
    w_core = [
        remote(wf.at[:, q], wf.at[:, q], ws_sem.at[1, 1 + i], wr_sem.at[1, 1 + i], mate)
        for i, q in enumerate((qi, over))
    ]

    w_near.start()

    @pl.when(middle * own_first == 1)
    def _():
        w_own.start()

    tell(step_sem.at[0])
    loads[0].wait()
    loads[1].wait()

    def first_tile(t, carry):
        a, j = t // row_tiles, t % row_tiles
        side = left[a, pl.ds(j * owners, owners)].reshape(tile, left.shape[4])
        prod = jnp.dot(side, tok[a], preferred_element_type=F32)
        first_s[a, pl.ds(j * per, per)] = prod.astype(BF16).reshape(per, ROWS, width)
        return carry

    first_tiles = blocks * row_tiles
    lax.fori_loop(0, first_tiles // 2, first_tile, 0)
    pl.semaphore_wait(step_sem.at[0], adjacent)
    tell(step_sem.at[1])
    lax.fori_loop(first_tiles // 2, first_tiles, first_tile, 0)

    def first_copy(k, t):
        peer = (me + t) % n
        return remote(
            first_s.at[:, peer * chunks + k], fc.at[k, pl.ds(me * blocks, blocks)],
            ssem.at[0, k, t], rsem.at[0, k, t], peer,
        )

    ahead = facing * PLANE + yi * 2

    @pl.when(middle == 1)
    def _():
        for c in range(2):
            first_copy(0, (ahead + c - me + n) % n).start()

    pl.semaphore_wait(step_sem.at[1], adjacent)
    tell(step_sem.at[2])
    pl.semaphore_wait(step_sem.at[2], adjacent)

    def send_first(k):
        def step(s, carry):
            t = (s * 7) % n
            peer = (me + t) % n
            done = middle * ((peer // 2 * 2 + n - ahead) % n == 0).astype(jnp.int32) if k == 0 else 0

            @pl.when(done == 0)
            def _():
                first_copy(k, t).start()

            return carry

        lax.fori_loop(1, n, step, 0)
        fc[k, pl.ds(me * blocks, blocks)] = first_s[:, me * chunks + k]

    def send_second_grad(k):
        each(functools.partial(to_cols, 1, k, sg_s, gc), "start")
        gc[k, pl.ds(me * blocks, blocks)] = sg_s[:, me * chunks + k]

    w_near.wait_recv()

    @pl.when(middle * (1 - own_first) == 1)
    def _():
        w_next.start()

    send_first(0)

    @pl.when(middle == 1)
    def _():
        w_got.wait_recv()
        w_group.start()
        w_group.wait_recv()
        w_pass.start()

    for k in range(1, chunks):
        send_first(k)

    loads[2].wait()

    @pl.when(middle == 1)
    def _():
        w_y.start()
        w_core[0].start()

    spread = (
        lax.broadcasted_iota(jnp.int32, (deep // ROWS, deep), 1) // ROWS
        == lax.broadcasted_iota(jnp.int32, (deep // ROWS, deep), 0)
    ).astype(F32).astype(BF16)
    same = (
        lax.broadcasted_iota(jnp.int32, (deep, deep), 0) % ROWS
        == lax.broadcasted_iota(jnp.int32, (deep, deep), 1) % ROWS
    )
    outer = deep // ROWS
    row = lax.broadcasted_iota(jnp.int32, (deep, deep), 0)
    col = lax.broadcasted_iota(jnp.int32, (deep, deep), 1)
    turn = ((row // ROWS == col % outer) & (row % ROWS == col // outer)).astype(F32).astype(BF16)
    loads[4].wait()
    for k in range(chunks):
        rk = jnp.dot(turn, right[k], preferred_element_type=F32).astype(BF16)
        wide = jnp.dot(rk, spread, preferred_element_type=F32)
        mix[k] = jnp.where(same, wide, 0.0).astype(BF16)

    def mixed(k, src, dst, dims):
        def step(t, carry):
            cols = pl.ds(pl.multiple_of(t * tile, tile), tile)
            x = src[k, :, :, cols].reshape(deep, tile)
            y = lax.dot_general(mix[k], x, (dims, ((), ())), preferred_element_type=F32)
            dst[k, :, :, cols] = y.astype(BF16).reshape(deep // ROWS, ROWS, tile)
            return carry

        lax.fori_loop(0, width // tile, step, 0)

    def second_of(k):
        each(functools.partial(to_cols, 0, k, first_s, fc), "recv")
        mixed(k, fc, sc, ((1,), (0,)))
        each(functools.partial(to_rows_, 2, k, sc, sr), "start")
        sr[:, k, me] = sc[k, pl.ds(me * blocks, blocks)]

    def first_grad_of(k):
        each(functools.partial(to_cols, 1, k, sg_s, gc), "recv")
        mixed(k, gc, fgc, ((0,), (0,)))
        each(functools.partial(to_rows_, 3, k, fgc, fr), "start")
        fr[:, k, me] = fgc[k, pl.ds(me * blocks, blocks)]

    second_of(0)

    @pl.when(middle == 0)
    def _():
        w_pass.wait_recv()
        w_y.start()
        w_core[0].start()

    w_y.wait_recv()
    w_core[1].start()
    for k in range(1, chunks):
        second_of(k)

    for copy in w_core:
        copy.wait_recv()
    loads[3].wait()

    def gate_tile(t, carry):
        a, j = t // row_tiles, t % row_tiles
        rows = pl.ds(j * tile, tile)
        weight = wf[...].reshape(width, width)
        g = jnp.dot(tok[a, rows, :], weight, preferred_element_type=F32).astype(BF16)
        gate[a, rows, :] = g
        gf = g.astype(F32)
        up = cot[a, rows, :].astype(F32) * (gf * jax.nn.sigmoid(gf))
        sg_s[a, pl.ds(j * per, per)] = up.astype(BF16).reshape(per, ROWS, width)
        return carry

    lax.fori_loop(0, blocks * row_tiles, gate_tile, 0)
    for k in range(chunks):
        send_second_grad(k)

    for k in range(chunks):
        each(functools.partial(to_rows_, 2, k, sc, sr), "recv")

    def delta_tile(t, carry):
        a, j = t // row_tiles, t % row_tiles
        rows = pl.ds(j * tile, tile)
        gf = gate[a, rows, :].astype(F32)
        sig = jax.nn.sigmoid(gf)
        sec = jnp.stack([sr[a, k, pl.ds(j * owners, owners)] for k in range(chunks)], axis=1)
        sec = sec.reshape(tile, width).astype(F32)
        up = cot[a, rows, :].astype(F32)
        out[a, rows, :] = (sec * (gf * sig)).astype(BF16)
        delta[a, rows, :] = (up * sec * (sig * (1.0 + gf * (1.0 - sig)))).astype(BF16)
        return carry

    lax.fori_loop(0, blocks * row_tiles, delta_tile, 0)
    def weight_tile(z, carry):
        cols = pl.ds(pl.multiple_of(z * tile, tile), tile)
        tokens_2d = tok[:, :, cols].reshape(blocks * tok.shape[1], tile)
        delta_2d = delta[...].reshape(blocks * tok.shape[1], width)
        prod = lax.dot_general(tokens_2d, delta_2d, (((0,), (0,)), ((), ())), preferred_element_type=F32)
        wt[z] = prod.astype(BF16).reshape(PLANE, tile // PLANE, width)
        return carry

    lax.fori_loop(0, width // tile, weight_tile, 0)

    g_core = [
        remote(wt.at[:, 2 * y + 1 - ci], half.at[y], gs_sem.at[0, y], gr_sem.at[0, y], mate) for y in range(2)
    ]
    g_y = remote(wt.at[:, over], half.at[2], gs_sem.at[0, 2], gr_sem.at[0, 2], zi * PLANE + over)
    g_near = [
        remote(quarter.at[beside], tail.at[0], gs_sem.at[1, 0], gr_sem.at[1, 0], beside * PLANE + qi),
        remote(
            quarter.at[(beside + nz // 2) % nz], tail.at[1], gs_sem.at[1, 1], gr_sem.at[1, 1], beside * PLANE + qi
        ),
    ]
    g_far = remote(pair, tail.at[2], gs_sem.at[1, 2], gr_sem.at[1, 2], across * PLANE + qi)

    for copy in g_core:
        copy.start()
    for copy in g_core:
        copy.wait_recv()

    def chip_tile(z, carry):
        wt[z, over] = (wt[z, over].astype(F32) + half[1 - yi, z].astype(F32)).astype(BF16)
        return carry

    lax.fori_loop(0, nz, chip_tile, 0)
    g_y.start()
    first_grad_of(0)
    g_y.wait_recv()

    def sum_tile(z, carry):
        total = wt[z, qi].astype(F32) + half[yi, z].astype(F32) + half[2, z].astype(F32)
        quarter[z] = total.astype(BF16)
        return carry

    lax.fori_loop(0, nz, sum_tile, 0)
    for copy in g_near:
        copy.start()
    def part_tile(t, carry):
        a, j = t // row_tiles, t % row_tiles
        rows = pl.ds(j * tile, tile)
        weight = wf[...].reshape(width, width)
        part[a, rows, :] = lax.dot_general(
            delta[a, rows, :], weight, (((1,), (1,)), ((), ())), preferred_element_type=F32
        )
        return carry

    lax.fori_loop(0, blocks * row_tiles, part_tile, 0)

    for copy in g_near:
        copy.wait_recv()
    pair[...] = (quarter[across].astype(F32) + tail[1].astype(F32)).astype(BF16)
    g_far.start()
    for k in range(1, chunks):
        first_grad_of(k)

    scale_w = width ** (-0.5)
    for k in range(chunks):
        pairs = lax.dot_general(
            gc[k].reshape(deep, width), fc[k].reshape(deep, width),
            (((1,), (1,)), ((), ())), preferred_element_type=F32,
        )
        kept = jnp.where(same, pairs * scale_w, 0.0).astype(BF16)
        picked = lax.dot_general(
            kept, spread, (((1,), (1,)), ((), ())), preferred_element_type=F32
        ).astype(BF16)
        rgrad[k] = lax.dot_general(
            turn, picked, (((0,), (0,)), ((), ())), preferred_element_type=F32
        ).astype(BF16)

    for k in range(chunks):
        each(functools.partial(to_cols, 0, k, first_s, fc), "send")
        each(functools.partial(to_rows_, 2, k, sc, sr), "send")
        each(functools.partial(to_cols, 1, k, sg_s, gc), "send")
    for copy in (w_near, w_y, *w_core, *g_core, g_y, *g_near):
        copy.wait_send()

    @pl.when(middle == 1)
    def _():
        for copy in (w_got, w_group, w_pass):
            copy.wait_send()

    for k in range(chunks - 1):
        each(functools.partial(to_rows_, 3, k, fgc, fr), "recv")

        def near_tile(t, carry):
            a, j = t // row_tiles, t % row_tiles
            rows = pl.ds(pl.multiple_of(j * tile, tile), tile)
            part[a, rows, :] += mixer_of(a, k, rows, left, fr)
            lgrad[a, k, :, :, rows] = left_grad_of(a, k, rows, tok, fr)
            return carry

        lax.fori_loop(0, blocks * row_tiles, near_tile, 0)
        each(functools.partial(to_rows_, 3, k, fgc, fr), "send")

    g_far.wait_recv()
    total = quarter[zi].astype(F32) + tail[0].astype(F32) + tail[2].astype(F32)
    ggrad[...] = total * (blocks * tok.shape[1] * n) ** (-0.5)
    g_far.wait_send()
    for k in range(chunks - 1, chunks):
        each(functools.partial(to_rows_, 3, k, fgc, fr), "send")
        each(functools.partial(to_rows_, 3, k, fgc, fr), "recv")


def mixer_of(a, k, rows, left, fr):
    high = fr.shape[2] * ROWS
    side = left[a, :, k, :, rows].reshape(high, rows.size)
    grad = fr[a, k].reshape(high, fr.shape[4])
    return lax.dot_general(side, grad, (((0,), (0,)), ((), ())), preferred_element_type=F32)


def left_grad_of(a, k, rows, tok, fr):
    high, width = fr.shape[2] * ROWS, fr.shape[4]
    grad = fr[a, k].reshape(high, width)
    lg = lax.dot_general(grad, tok[a, rows, :], (((1,), (1,)), ((), ())), preferred_element_type=F32)
    return (lg * width ** (-0.5)).astype(BF16).reshape(fr.shape[2], ROWS, rows.size)


def last_kernel(
    tok, left, out_in, part, fr, lgrad_in, ggrad_in, rgrad_in,
    out, igrad, lgrad, ggrad, rgrad,
    ig, lg, sem, ig_sem, lg_sem,
):
    blocks, chunks = fr.shape[0], fr.shape[1]
    tile = 256
    last = chunks - 1
    copies = [
        pltpu.make_async_copy(out_in, out, sem.at[0]),
        pltpu.make_async_copy(ggrad_in, ggrad, sem.at[1]),
        pltpu.make_async_copy(rgrad_in, rgrad, sem.at[2]),
    ]
    for k in range(last):
        copies.append(pltpu.make_async_copy(lgrad_in.at[:, k], lgrad.at[:, :, k], sem.at[3 + k]))
    for copy in copies:
        copy.start()
    for a in range(blocks):
        for j in range(tok.shape[1] // tile):
            rows = pl.ds(j * tile, tile)
            lg[a, :, :, rows] = left_grad_of(a, last, rows, tok, fr)
            if j == tok.shape[1] // tile - 1:
                copy = pltpu.make_async_copy(lg.at[a], lgrad.at[a, :, last], lg_sem.at[a])
                copy.start()
                copies.append(copy)
            ig[a, rows, :] = (part[a, rows, :] + mixer_of(a, last, rows, left, fr)).astype(BF16)
            copy = pltpu.make_async_copy(ig.at[a, rows], igrad.at[a, rows], ig_sem.at[a, j])
            copy.start()
            copies.append(copy)
    for copy in copies:
        copy.wait()


def fused_body(n, tokens, cotangent, gate_weight, left_blocks, right_blocks):
    blocks, inner = left_blocks.shape[0], left_blocks.shape[1]
    own, outer = right_blocks.shape[0], right_blocks.shape[1]
    width = tokens.shape[1]
    chunks = own // ROWS
    groups = inner // ROWS
    deep = outer * ROWS
    nz = n // PLANE
    shard = width // n
    rows = (blocks, inner, width)
    split = (blocks, n, chunks, ROWS, inner)
    near = (blocks, chunks - 1, n, ROWS, inner)
    by_row = pltpu.VMEM((blocks, groups, ROWS, width), BF16)
    by_owner = (blocks, chunks, n, ROWS, width)
    by_col = pltpu.VMEM((chunks, outer, ROWS, width), BF16)
    vmem = pl.BlockSpec(memory_space=pltpu.VMEM)
    hbm = pl.BlockSpec(memory_space=pltpu.HBM)
    args = (
        tokens.reshape(rows), cotangent.reshape(rows), gate_weight, left_blocks.reshape(split),
        right_blocks.reshape(chunks, deep, outer),
    )
    kept = pl.pallas_call(
        functools.partial(mixer_kernel, n),
        out_shape=(
            pltpu.VMEM(rows, BF16),
            pltpu.VMEM(split, BF16),
            pltpu.VMEM(rows, BF16),
            pltpu.VMEM(rows, F32),
            pltpu.VMEM(by_owner, BF16),
            pltpu.VMEM(near, BF16),
            pltpu.VMEM((shard, width), F32),
            pltpu.VMEM((chunks, deep, outer), BF16),
        ),
        in_specs=[hbm] * 5,
        out_specs=[vmem] * 8,
        scratch_shapes=[
            pltpu.VMEM((chunks, deep, outer), BF16),
            pltpu.VMEM(rows, BF16),
            pltpu.VMEM((nz, PLANE, shard, width), BF16),
            by_row, by_row, by_col, by_col, by_col, by_col, pltpu.VMEM(by_owner, BF16),
            pltpu.VMEM(rows, BF16),
            pltpu.VMEM(rows, BF16),
            pltpu.VMEM((nz, PLANE, shard, width), BF16),
            pltpu.VMEM((PLANE - 1, nz, shard, width), BF16),
            pltpu.VMEM((nz, shard, width), BF16),
            pltpu.VMEM((shard, width), BF16),
            pltpu.VMEM((3, shard, width), BF16),
            pltpu.VMEM((chunks, deep, deep), BF16),
            pltpu.SemaphoreType.DMA((4, chunks, n)),
            pltpu.SemaphoreType.DMA((4, chunks, n)),
            pltpu.SemaphoreType.DMA((2, PLANE)),
            pltpu.SemaphoreType.DMA((2, PLANE)),
            pltpu.SemaphoreType.DMA((2, PLANE)),
            pltpu.SemaphoreType.DMA((2, PLANE)),
            pltpu.SemaphoreType.DMA((5,)),
            pltpu.SemaphoreType.REGULAR((3,)),
        ],
        compiler_params=pltpu.CompilerParams(
            collective_id=0, has_side_effects=True, vmem_limit_bytes=36 * 2**20
        ),
    )(*[pltpu.with_memory_space_constraint(x, pltpu.HBM) for x in args])
    out, igrad, lgrad, ggrad, rgrad = pl.pallas_call(
        last_kernel,
        out_shape=(
            jax.ShapeDtypeStruct(rows, BF16),
            jax.ShapeDtypeStruct(rows, BF16),
            jax.ShapeDtypeStruct(split, BF16),
            jax.ShapeDtypeStruct((shard, width), F32),
            jax.ShapeDtypeStruct((chunks, deep, outer), BF16),
        ),
        in_specs=[vmem] * 8,
        out_specs=[hbm] * 5,
        scratch_shapes=[
            pltpu.VMEM(rows, BF16),
            pltpu.VMEM((blocks, n, ROWS, inner), BF16),
            pltpu.SemaphoreType.DMA((2 + chunks,)),
            pltpu.SemaphoreType.DMA((blocks, inner // 256)),
            pltpu.SemaphoreType.DMA((blocks,)),
        ],
        compiler_params=pltpu.CompilerParams(vmem_limit_bytes=12 * 2**20),
    )(*[pltpu.with_memory_space_constraint(x, pltpu.VMEM) for x in kept])
    return (
        out.reshape(tokens.shape), igrad.reshape(tokens.shape), ggrad, lgrad.reshape(left_blocks.shape),
        rgrad.reshape(own, outer, outer),
    )


def chosen_body(tokens, cotangent, gate_weight, left_blocks, right_blocks):
    n = lax.axis_size("seq")
    own, width, inner = right_blocks.shape[0], tokens.shape[1], left_blocks.shape[1]
    if lax.axis_size("groups") == 2 and n == PLANE * PLANE and own % ROWS == 0 and width == 256 * PLANE and inner % 256 == 0:
        return fused_body(n, tokens, cotangent, gate_weight, left_blocks, right_blocks)
    return body(tokens, cotangent, gate_weight, left_blocks, right_blocks)


def solution(mesh):
    in_specs = (
        P(("groups", "seq"), None),
        P(("groups", "seq"), None),
        P("seq", None),
        P("seq", None, None),
        P("seq", None, None),
    )
    out_specs = (
        P(("groups", "seq"), None),
        P(("groups", "seq"), None),
        P(("groups", "seq"), None),
        P(("groups", "seq"), None, None),
        P(("groups", "seq"), None, None),
    )
    return jax.shard_map(chosen_body, mesh=mesh, in_specs=in_specs, out_specs=out_specs, check_vma=False)
```

```python
import functools

import jax
import jax.numpy as jnp
from jax import lax
from jax.experimental import pallas as pl
from jax.experimental.pallas import tpu as pltpu
from jax.sharding import PartitionSpec as P


def silu_slope(value):
    sig = jax.nn.sigmoid(value)
    return sig * (1.0 + value * (1.0 - sig))


def to_columns(values):
    return lax.all_to_all(values, "seq", split_axis=1, concat_axis=0, tiled=True)


def to_rows(values):
    return lax.all_to_all(values, "seq", split_axis=0, concat_axis=1, tiled=True)


def body(tokens, cotangent, gate_weight, left_blocks, right_blocks):
    seq_count = lax.axis_size("seq")
    local_blocks = left_blocks.shape[0]
    block_size = left_blocks.shape[1]
    tok_rows = tokens.shape[0]
    channels = tokens.shape[1]
    token_grid = tokens.reshape(local_blocks, block_size, channels)
    upstream = cotangent.reshape(local_blocks, block_size, channels)
    first = jnp.einsum(
        "ajb,abc->ajc", left_blocks, token_grid, preferred_element_type=jnp.float32
    ).astype(jnp.bfloat16)
    full_weight = lax.all_gather(gate_weight, "seq", axis=0, tiled=True)
    gate_sum = jnp.dot(tokens, full_weight, preferred_element_type=jnp.float32)
    gate = gate_sum.astype(jnp.bfloat16).reshape(local_blocks, block_size, channels)
    first_cols = to_columns(first)
    second_cols = jnp.einsum(
        "bia,abc->ibc", right_blocks, first_cols, preferred_element_type=jnp.float32
    ).astype(jnp.bfloat16)
    second = to_rows(second_cols)
    gate_f = gate.astype(jnp.float32)
    factor = jax.nn.silu(gate_f)
    second_f = second.astype(jnp.float32)
    upstream_f = upstream.astype(jnp.float32)
    output = (second_f * factor).astype(jnp.bfloat16)
    second_grad = (upstream_f * factor).astype(jnp.bfloat16)
    gate_delta = (upstream_f * second_f * silu_slope(gate_f)).astype(jnp.bfloat16)
    grad_cols = to_columns(second_grad)
    first_grad_cols = jnp.einsum(
        "bia,ibc->abc", right_blocks, grad_cols, preferred_element_type=jnp.float32
    ).astype(jnp.bfloat16)
    scale_w = channels ** (-0.5)
    right_grad = (
        jnp.einsum("ibc,abc->bia", grad_cols, first_cols, preferred_element_type=jnp.float32)
        * scale_w
    ).astype(jnp.bfloat16)
    first_grad = to_rows(first_grad_cols)
    left_grad = (
        jnp.einsum("ajc,abc->ajb", first_grad, token_grid, preferred_element_type=jnp.float32)
        * scale_w
    ).astype(jnp.bfloat16)
    mixer_part = jnp.einsum(
        "ajb,ajc->abc", left_blocks, first_grad, preferred_element_type=jnp.float32
    ).reshape(tok_rows, channels)
    delta_flat = gate_delta.reshape(tok_rows, channels)
    gate_part = jnp.einsum("tc,kc->tk", delta_flat, full_weight, preferred_element_type=jnp.float32)
    input_grad = (mixer_part + gate_part).astype(jnp.bfloat16)
    weight_term = jnp.einsum("tk,tc->kc", tokens, delta_flat, preferred_element_type=jnp.float32)
    gate_grad = lax.psum_scatter(weight_term, "seq", scatter_dimension=0, tiled=True)
    gate_grad = gate_grad * (tok_rows * seq_count) ** (-0.5)
    return (output.reshape(tok_rows, channels), input_grad, gate_grad, left_grad, right_grad)


F32 = jnp.float32
BF16 = jnp.bfloat16
ROWS = 16
PLANE = 4


def mixer_kernel(
    n, tok_hbm, cot_hbm, wsh, left_hbm, right_hbm,
    tok, left, out, part, fr, lgrad, ggrad, rgrad,
    right, cot, wf, first_s, sg_s, fc, gc, sc, fgc, sr, gate, delta, wt, half, quarter, pair, tail, mix,
    ssem, rsem, ws_sem, wr_sem, gs_sem, gr_sem, lsem, step_sem,
):
    me = lax.axis_index("seq")
    zi, qi = me // PLANE, me % PLANE
    chunks = fc.shape[0]
    blocks, width = tok.shape[0], tok.shape[2]
    nz = n // PLANE
    deep = fc.shape[1] * ROWS
    tile = 256
    per = tile // ROWS
    row_tiles = tok.shape[1] // tile
    owners = per // chunks

    loads = [
        pltpu.make_async_copy(left_hbm, left, lsem.at[0]),
        pltpu.make_async_copy(tok_hbm, tok, lsem.at[1]),
        pltpu.make_async_copy(wsh, wf.at[zi, qi], lsem.at[2]),
        pltpu.make_async_copy(cot_hbm, cot, lsem.at[3]),
        pltpu.make_async_copy(right_hbm, right, lsem.at[4]),
    ]

    gi = lax.axis_index("groups")
    yi, ci = qi // 2, qi % 2
    middle = ((zi + 1) // 2) % 2
    adjacent = 5 + 2 * middle
    facing = nz - 1 - zi

    def tell(sem):
        def signal(dev):
            pl.semaphore_signal(sem, inc=1, device_id={"seq": dev}, device_id_type=pl.DeviceIdType.MESH)

        signal(me + 1 - 2 * ci)
        for c in range(2):
            signal(zi * PLANE + (1 - yi) * 2 + c)
            pl.when(zi > 0)(functools.partial(signal, (zi - 1) * PLANE + yi * 2 + c))
            pl.when(zi < nz - 1)(functools.partial(signal, (zi + 1) * PLANE + yi * 2 + c))

    barrier = pltpu.get_barrier_semaphore()
    pl.semaphore_signal(barrier, inc=1, device_id={"groups": 1 - gi}, device_id_type=pl.DeviceIdType.MESH)
    tell(barrier)
    for load in loads:
        load.start()
    pl.semaphore_wait(barrier, adjacent + 1)

    def remote(src, dst, ss, rs, dev):
        return pltpu.make_async_remote_copy(
            src_ref=src, dst_ref=dst, send_sem=ss, recv_sem=rs,
            device_id={"seq": dev}, device_id_type=pl.DeviceIdType.MESH,
        )

    def to_cols(ph, k, src, dst, s):
        t = s % n
        peer = (me + t) % n
        return remote(
            src.at[:, peer * chunks + k], dst.at[k, pl.ds(me * blocks, blocks)],
            ssem.at[ph, k, t], rsem.at[ph, k, t], peer,
        )

    def to_rows_(ph, k, src, dst, s):
        t = s % n
        peer = (me + t) % n
        return remote(
            src.at[k, pl.ds(peer * blocks, blocks)], dst.at[:, k, me],
            ssem.at[ph, k, t], rsem.at[ph, k, t], peer,
        )

    def each(make, action):
        def step(s, carry):
            copy = make(s)
            if action == "start":
                copy.start()
            elif action == "recv":
                copy.wait_recv()
            else:
                copy.wait_send()
            return carry

        lax.fori_loop(1, n, step, 0)

    across = (zi + nz // 2) % nz
    beside = zi + 1 - 2 * (zi % 2)
    own_first = (ci + gi + 1) % 2
    carried = facing * own_first + across * (1 - own_first)
    other_half = pl.ds((1 - zi // 2) * 2, 2)

    w_near = remote(wsh, wf.at[zi, qi], ws_sem.at[0, 1], wr_sem.at[0, 1], beside * PLANE + qi)
    w_own = remote(wsh, wf.at[zi, qi], ws_sem.at[0, 0], wr_sem.at[0, 0], facing * PLANE + qi)
    w_next = remote(wf.at[beside, qi], wf.at[beside, qi], ws_sem.at[0, 0], wr_sem.at[0, 0], facing * PLANE + qi)
    w_got = remote(wf.at[carried, qi], wf.at[carried, qi], ws_sem.at[0, 0], wr_sem.at[0, 0], facing * PLANE + qi)
    w_group = pltpu.make_async_remote_copy(
        src_ref=wf.at[carried, qi], dst_ref=wf.at[carried, qi], send_sem=ws_sem.at[0, 3], recv_sem=wr_sem.at[0, 3],
        device_id={"groups": 1 - gi}, device_id_type=pl.DeviceIdType.MESH,
    )
    w_pass = remote(
        wf.at[other_half, qi], wf.at[other_half, qi], ws_sem.at[0, 2], wr_sem.at[0, 2], beside * PLANE + qi
    )

    mate = me + 1 - 2 * ci
    over = (1 - yi) * 2 + ci
    w_y = remote(wf.at[:, qi], wf.at[:, qi], ws_sem.at[1, 0], wr_sem.at[1, 0], zi * PLANE + over)
    w_core = [
        remote(wf.at[:, q], wf.at[:, q], ws_sem.at[1, 1 + i], wr_sem.at[1, 1 + i], mate)
        for i, q in enumerate((qi, over))
    ]

    w_near.start()

    @pl.when(middle * own_first == 1)
    def _():
        w_own.start()

    tell(step_sem.at[0])
    loads[0].wait()
    loads[1].wait()

    def first_tile(t, carry):
        a, j = t // row_tiles, t % row_tiles
        side = left[a, pl.ds(j * owners, owners)].reshape(tile, left.shape[4])
        prod = jnp.dot(side, tok[a], preferred_element_type=F32)
        first_s[a, pl.ds(j * per, per)] = prod.astype(BF16).reshape(per, ROWS, width)
        return carry

    first_tiles = blocks * row_tiles
    lax.fori_loop(0, first_tiles // 2, first_tile, 0)
    pl.semaphore_wait(step_sem.at[0], adjacent)
    tell(step_sem.at[1])
    lax.fori_loop(first_tiles // 2, first_tiles, first_tile, 0)

    def first_copy(k, t):
        peer = (me + t) % n
        return remote(
            first_s.at[:, peer * chunks + k], fc.at[k, pl.ds(me * blocks, blocks)],
            ssem.at[0, k, t], rsem.at[0, k, t], peer,
        )

    ahead = facing * PLANE + yi * 2

    @pl.when(middle == 1)
    def _():
        for c in range(2):
            first_copy(0, (ahead + c - me + n) % n).start()

    pl.semaphore_wait(step_sem.at[1], adjacent)
    tell(step_sem.at[2])

    @pl.when(middle == 0)
    def _():
        pl.semaphore_wait(step_sem.at[2], adjacent)


    def send_first(k):
        def step(s, carry):
            t = s % n
            peer = (me + t) % n
            done = middle * ((peer // 2 * 2 + n - ahead) % n == 0).astype(jnp.int32) if k == 0 else 0

            @pl.when(done == 0)
            def _():
                first_copy(k, t).start()

            return carry

        lax.fori_loop(1, n, step, 0)
        fc[k, pl.ds(me * blocks, blocks)] = first_s[:, me * chunks + k]

    def send_second_grad(k):
        each(functools.partial(to_cols, 1, k, sg_s, gc), "start")
        gc[k, pl.ds(me * blocks, blocks)] = sg_s[:, me * chunks + k]

    w_near.wait_recv()

    @pl.when(middle * (1 - own_first) == 1)
    def _():
        w_next.start()

    send_first(0)

    @pl.when(middle == 1)
    def _():
        pl.semaphore_wait(step_sem.at[2], adjacent)


    @pl.when(middle == 1)
    def _():
        w_got.wait_recv()
        w_group.start()
        w_group.wait_recv()
        w_pass.start()

    for k in range(1, chunks):
        send_first(k)

    loads[2].wait()

    @pl.when(middle == 1)
    def _():
        w_y.start()
        w_core[0].start()

    spread = (
        lax.broadcasted_iota(jnp.int32, (deep // ROWS, deep), 1) // ROWS
        == lax.broadcasted_iota(jnp.int32, (deep // ROWS, deep), 0)
    ).astype(F32).astype(BF16)
    same = (
        lax.broadcasted_iota(jnp.int32, (deep, deep), 0) % ROWS
        == lax.broadcasted_iota(jnp.int32, (deep, deep), 1) % ROWS
    )
    outer = deep // ROWS
    row = lax.broadcasted_iota(jnp.int32, (deep, deep), 0)
    col = lax.broadcasted_iota(jnp.int32, (deep, deep), 1)
    turn = ((row // ROWS == col % outer) & (row % ROWS == col // outer)).astype(F32).astype(BF16)
    loads[4].wait()
    for k in range(chunks):
        rk = jnp.dot(turn, right[k], preferred_element_type=F32).astype(BF16)
        wide = jnp.dot(rk, spread, preferred_element_type=F32)
        mix[k] = jnp.where(same, wide, 0.0).astype(BF16)

    def mixed(k, src, dst, dims):
        def step(t, carry):
            cols = pl.ds(pl.multiple_of(t * tile, tile), tile)
            x = src[k, :, :, cols].reshape(deep, tile)
            y = lax.dot_general(mix[k], x, (dims, ((), ())), preferred_element_type=F32)
            dst[k, :, :, cols] = y.astype(BF16).reshape(deep // ROWS, ROWS, tile)
            return carry

        lax.fori_loop(0, width // tile, step, 0)

    def second_of(k):
        each(functools.partial(to_cols, 0, k, first_s, fc), "recv")
        mixed(k, fc, sc, ((1,), (0,)))
        each(functools.partial(to_rows_, 2, k, sc, sr), "start")
        sr[:, k, me] = sc[k, pl.ds(me * blocks, blocks)]

    def first_grad_of(k):
        each(functools.partial(to_cols, 1, k, sg_s, gc), "recv")
        mixed(k, gc, fgc, ((0,), (0,)))
        each(functools.partial(to_rows_, 3, k, fgc, fr), "start")
        fr[:, k, me] = fgc[k, pl.ds(me * blocks, blocks)]

    second_of(0)

    @pl.when(middle == 0)
    def _():
        w_pass.wait_recv()
        w_y.start()
        w_core[0].start()

    w_y.wait_recv()
    w_core[1].start()
    for k in range(1, chunks):
        second_of(k)

    for copy in w_core:
        copy.wait_recv()
    loads[3].wait()

    def gate_tile(t, carry):
        a, j = t // row_tiles, t % row_tiles
        rows = pl.ds(j * tile, tile)
        weight = wf[...].reshape(width, width)
        g = jnp.dot(tok[a, rows, :], weight, preferred_element_type=F32).astype(BF16)
        gate[a, rows, :] = g
        gf = g.astype(F32)
        up = cot[a, rows, :].astype(F32) * (gf * jax.nn.sigmoid(gf))
        sg_s[a, pl.ds(j * per, per)] = up.astype(BF16).reshape(per, ROWS, width)
        return carry

    lax.fori_loop(0, blocks * row_tiles, gate_tile, 0)
    for k in range(chunks):
        send_second_grad(k)

    for k in range(chunks):
        each(functools.partial(to_rows_, 2, k, sc, sr), "recv")

    def delta_tile(t, carry):
        a, j = t // row_tiles, t % row_tiles
        rows = pl.ds(j * tile, tile)
        gf = gate[a, rows, :].astype(F32)
        sig = jax.nn.sigmoid(gf)
        sec = jnp.stack([sr[a, k, pl.ds(j * owners, owners)] for k in range(chunks)], axis=1)
        sec = sec.reshape(tile, width).astype(F32)
        up = cot[a, rows, :].astype(F32)
        out[a, rows, :] = (sec * (gf * sig)).astype(BF16)
        delta[a, rows, :] = (up * sec * (sig * (1.0 + gf * (1.0 - sig)))).astype(BF16)
        return carry

    lax.fori_loop(0, blocks * row_tiles, delta_tile, 0)
    def weight_tile(z, carry):
        cols = pl.ds(pl.multiple_of(z * tile, tile), tile)
        tokens_2d = tok[:, :, cols].reshape(blocks * tok.shape[1], tile)
        delta_2d = delta[...].reshape(blocks * tok.shape[1], width)
        prod = lax.dot_general(tokens_2d, delta_2d, (((0,), (0,)), ((), ())), preferred_element_type=F32)
        wt[z] = prod.astype(BF16).reshape(PLANE, tile // PLANE, width)
        return carry

    lax.fori_loop(0, width // tile, weight_tile, 0)

    g_core = [
        remote(wt.at[:, 2 * y + 1 - ci], half.at[y], gs_sem.at[0, y], gr_sem.at[0, y], mate) for y in range(2)
    ]
    g_y = remote(wt.at[:, over], half.at[2], gs_sem.at[0, 2], gr_sem.at[0, 2], zi * PLANE + over)
    g_near = [
        remote(quarter.at[beside], tail.at[0], gs_sem.at[1, 0], gr_sem.at[1, 0], beside * PLANE + qi),
        remote(
            quarter.at[(beside + nz // 2) % nz], tail.at[1], gs_sem.at[1, 1], gr_sem.at[1, 1], beside * PLANE + qi
        ),
    ]
    g_far = remote(pair, tail.at[2], gs_sem.at[1, 2], gr_sem.at[1, 2], across * PLANE + qi)

    for copy in g_core:
        copy.start()
    for copy in g_core:
        copy.wait_recv()

    def chip_tile(z, carry):
        wt[z, over] = (wt[z, over].astype(F32) + half[1 - yi, z].astype(F32)).astype(BF16)
        return carry

    lax.fori_loop(0, nz, chip_tile, 0)
    g_y.start()
    first_grad_of(0)
    g_y.wait_recv()

    def sum_tile(z, carry):
        total = wt[z, qi].astype(F32) + half[yi, z].astype(F32) + half[2, z].astype(F32)
        quarter[z] = total.astype(BF16)
        return carry

    lax.fori_loop(0, nz, sum_tile, 0)
    for copy in g_near:
        copy.start()
    def part_tile(t, carry):
        a, j = t // row_tiles, t % row_tiles
        rows = pl.ds(j * tile, tile)
        weight = wf[...].reshape(width, width)
        part[a, rows, :] = lax.dot_general(
            delta[a, rows, :], weight, (((1,), (1,)), ((), ())), preferred_element_type=F32
        )
        return carry

    lax.fori_loop(0, blocks * row_tiles, part_tile, 0)

    for copy in g_near:
        copy.wait_recv()
    pair[...] = (quarter[across].astype(F32) + tail[1].astype(F32)).astype(BF16)
    g_far.start()
    for k in range(1, chunks):
        first_grad_of(k)

    scale_w = width ** (-0.5)
    for k in range(chunks):
        pairs = lax.dot_general(
            gc[k].reshape(deep, width), fc[k].reshape(deep, width),
            (((1,), (1,)), ((), ())), preferred_element_type=F32,
        )
        kept = jnp.where(same, pairs * scale_w, 0.0).astype(BF16)
        picked = lax.dot_general(
            kept, spread, (((1,), (1,)), ((), ())), preferred_element_type=F32
        ).astype(BF16)
        rgrad[k] = lax.dot_general(
            turn, picked, (((0,), (0,)), ((), ())), preferred_element_type=F32
        ).astype(BF16)

    for k in range(chunks):
        each(functools.partial(to_cols, 0, k, first_s, fc), "send")
        each(functools.partial(to_rows_, 2, k, sc, sr), "send")
        each(functools.partial(to_cols, 1, k, sg_s, gc), "send")
    for copy in (w_near, w_y, *w_core, *g_core, g_y, *g_near):
        copy.wait_send()

    @pl.when(middle == 1)
    def _():
        for copy in (w_got, w_group, w_pass):
            copy.wait_send()

    for k in range(chunks - 1):
        each(functools.partial(to_rows_, 3, k, fgc, fr), "recv")

        def near_tile(t, carry):
            a, j = t // row_tiles, t % row_tiles
            rows = pl.ds(pl.multiple_of(j * tile, tile), tile)
            part[a, rows, :] += mixer_of(a, k, rows, left, fr)
            lgrad[a, k, :, :, rows] = left_grad_of(a, k, rows, tok, fr)
            return carry

        lax.fori_loop(0, blocks * row_tiles, near_tile, 0)
        each(functools.partial(to_rows_, 3, k, fgc, fr), "send")

    g_far.wait_recv()
    total = quarter[zi].astype(F32) + tail[0].astype(F32) + tail[2].astype(F32)
    ggrad[...] = total * (blocks * tok.shape[1] * n) ** (-0.5)
    g_far.wait_send()
    for k in range(chunks - 1, chunks):
        each(functools.partial(to_rows_, 3, k, fgc, fr), "send")
        each(functools.partial(to_rows_, 3, k, fgc, fr), "recv")


def mixer_of(a, k, rows, left, fr):
    high = fr.shape[2] * ROWS
    side = left[a, :, k, :, rows].reshape(high, rows.size)
    grad = fr[a, k].reshape(high, fr.shape[4])
    return lax.dot_general(side, grad, (((0,), (0,)), ((), ())), preferred_element_type=F32)


def left_grad_of(a, k, rows, tok, fr):
    high, width = fr.shape[2] * ROWS, fr.shape[4]
    grad = fr[a, k].reshape(high, width)
    lg = lax.dot_general(grad, tok[a, rows, :], (((1,), (1,)), ((), ())), preferred_element_type=F32)
    return (lg * width ** (-0.5)).astype(BF16).reshape(fr.shape[2], ROWS, rows.size)


def last_kernel(
    tok, left, out_in, part, fr, lgrad_in, ggrad_in, rgrad_in,
    out, igrad, lgrad, ggrad, rgrad,
    ig, lg, sem, ig_sem, lg_sem,
):
    blocks, chunks = fr.shape[0], fr.shape[1]
    tile = 256
    last = chunks - 1
    copies = [
        pltpu.make_async_copy(out_in, out, sem.at[0]),
        pltpu.make_async_copy(ggrad_in, ggrad, sem.at[1]),
        pltpu.make_async_copy(rgrad_in, rgrad, sem.at[2]),
    ]
    for k in range(last):
        copies.append(pltpu.make_async_copy(lgrad_in.at[:, k], lgrad.at[:, :, k], sem.at[3 + k]))
    for copy in copies:
        copy.start()
    for a in range(blocks):
        for j in range(tok.shape[1] // tile):
            rows = pl.ds(j * tile, tile)
            lg[a, :, :, rows] = left_grad_of(a, last, rows, tok, fr)
            if j == tok.shape[1] // tile - 1:
                copy = pltpu.make_async_copy(lg.at[a], lgrad.at[a, :, last], lg_sem.at[a])
                copy.start()
                copies.append(copy)
            ig[a, rows, :] = (part[a, rows, :] + mixer_of(a, last, rows, left, fr)).astype(BF16)
            copy = pltpu.make_async_copy(ig.at[a, rows], igrad.at[a, rows], ig_sem.at[a, j])
            copy.start()
            copies.append(copy)
    for copy in copies:
        copy.wait()


def fused_body(n, tokens, cotangent, gate_weight, left_blocks, right_blocks):
    blocks, inner = left_blocks.shape[0], left_blocks.shape[1]
    own, outer = right_blocks.shape[0], right_blocks.shape[1]
    width = tokens.shape[1]
    chunks = own // ROWS
    groups = inner // ROWS
    deep = outer * ROWS
    nz = n // PLANE
    shard = width // n
    rows = (blocks, inner, width)
    split = (blocks, n, chunks, ROWS, inner)
    near = (blocks, chunks - 1, n, ROWS, inner)
    by_row = pltpu.VMEM((blocks, groups, ROWS, width), BF16)
    by_owner = (blocks, chunks, n, ROWS, width)
    by_col = pltpu.VMEM((chunks, outer, ROWS, width), BF16)
    vmem = pl.BlockSpec(memory_space=pltpu.VMEM)
    hbm = pl.BlockSpec(memory_space=pltpu.HBM)
    args = (
        tokens.reshape(rows), cotangent.reshape(rows), gate_weight, left_blocks.reshape(split),
        right_blocks.reshape(chunks, deep, outer),
    )
    kept = pl.pallas_call(
        functools.partial(mixer_kernel, n),
        out_shape=(
            pltpu.VMEM(rows, BF16),
            pltpu.VMEM(split, BF16),
            pltpu.VMEM(rows, BF16),
            pltpu.VMEM(rows, F32),
            pltpu.VMEM(by_owner, BF16),
            pltpu.VMEM(near, BF16),
            pltpu.VMEM((shard, width), F32),
            pltpu.VMEM((chunks, deep, outer), BF16),
        ),
        in_specs=[hbm] * 5,
        out_specs=[vmem] * 8,
        scratch_shapes=[
            pltpu.VMEM((chunks, deep, outer), BF16),
            pltpu.VMEM(rows, BF16),
            pltpu.VMEM((nz, PLANE, shard, width), BF16),
            by_row, by_row, by_col, by_col, by_col, by_col, pltpu.VMEM(by_owner, BF16),
            pltpu.VMEM(rows, BF16),
            pltpu.VMEM(rows, BF16),
            pltpu.VMEM((nz, PLANE, shard, width), BF16),
            pltpu.VMEM((PLANE - 1, nz, shard, width), BF16),
            pltpu.VMEM((nz, shard, width), BF16),
            pltpu.VMEM((shard, width), BF16),
            pltpu.VMEM((3, shard, width), BF16),
            pltpu.VMEM((chunks, deep, deep), BF16),
            pltpu.SemaphoreType.DMA((4, chunks, n)),
            pltpu.SemaphoreType.DMA((4, chunks, n)),
            pltpu.SemaphoreType.DMA((2, PLANE)),
            pltpu.SemaphoreType.DMA((2, PLANE)),
            pltpu.SemaphoreType.DMA((2, PLANE)),
            pltpu.SemaphoreType.DMA((2, PLANE)),
            pltpu.SemaphoreType.DMA((5,)),
            pltpu.SemaphoreType.REGULAR((3,)),
        ],
        compiler_params=pltpu.CompilerParams(
            collective_id=0, has_side_effects=True, vmem_limit_bytes=36 * 2**20
        ),
    )(*[pltpu.with_memory_space_constraint(x, pltpu.HBM) for x in args])
    out, igrad, lgrad, ggrad, rgrad = pl.pallas_call(
        last_kernel,
        out_shape=(
            jax.ShapeDtypeStruct(rows, BF16),
            jax.ShapeDtypeStruct(rows, BF16),
            jax.ShapeDtypeStruct(split, BF16),
            jax.ShapeDtypeStruct((shard, width), F32),
            jax.ShapeDtypeStruct((chunks, deep, outer), BF16),
        ),
        in_specs=[vmem] * 8,
        out_specs=[hbm] * 5,
        scratch_shapes=[
            pltpu.VMEM(rows, BF16),
            pltpu.VMEM((blocks, n, ROWS, inner), BF16),
            pltpu.SemaphoreType.DMA((2 + chunks,)),
            pltpu.SemaphoreType.DMA((blocks, inner // 256)),
            pltpu.SemaphoreType.DMA((blocks,)),
        ],
        compiler_params=pltpu.CompilerParams(vmem_limit_bytes=12 * 2**20),
    )(*[pltpu.with_memory_space_constraint(x, pltpu.VMEM) for x in kept])
    return (
        out.reshape(tokens.shape), igrad.reshape(tokens.shape), ggrad, lgrad.reshape(left_blocks.shape),
        rgrad.reshape(own, outer, outer),
    )


def chosen_body(tokens, cotangent, gate_weight, left_blocks, right_blocks):
    n = lax.axis_size("seq")
    own, width, inner = right_blocks.shape[0], tokens.shape[1], left_blocks.shape[1]
    if lax.axis_size("groups") == 2 and n == PLANE * PLANE and own % ROWS == 0 and width == 256 * PLANE and inner % 256 == 0:
        return fused_body(n, tokens, cotangent, gate_weight, left_blocks, right_blocks)
    return body(tokens, cotangent, gate_weight, left_blocks, right_blocks)


def solution(mesh):
    in_specs = (
        P(("groups", "seq"), None),
        P(("groups", "seq"), None),
        P("seq", None),
        P("seq", None, None),
        P("seq", None, None),
    )
    out_specs = (
        P(("groups", "seq"), None),
        P(("groups", "seq"), None),
        P(("groups", "seq"), None),
        P(("groups", "seq"), None, None),
        P(("groups", "seq"), None, None),
    )
    return jax.shard_map(chosen_body, mesh=mesh, in_specs=in_specs, out_specs=out_specs, check_vma=False)
```

```python
import functools

import jax
import jax.numpy as jnp
from jax import lax
from jax.experimental import pallas as pl
from jax.experimental.pallas import tpu as pltpu
from jax.sharding import PartitionSpec as P


def silu_slope(value):
    sig = jax.nn.sigmoid(value)
    return sig * (1.0 + value * (1.0 - sig))


def to_columns(values):
    return lax.all_to_all(values, "seq", split_axis=1, concat_axis=0, tiled=True)


def to_rows(values):
    return lax.all_to_all(values, "seq", split_axis=0, concat_axis=1, tiled=True)


def body(tokens, cotangent, gate_weight, left_blocks, right_blocks):
    seq_count = lax.axis_size("seq")
    local_blocks = left_blocks.shape[0]
    block_size = left_blocks.shape[1]
    tok_rows = tokens.shape[0]
    channels = tokens.shape[1]
    token_grid = tokens.reshape(local_blocks, block_size, channels)
    upstream = cotangent.reshape(local_blocks, block_size, channels)
    first = jnp.einsum(
        "ajb,abc->ajc", left_blocks, token_grid, preferred_element_type=jnp.float32
    ).astype(jnp.bfloat16)
    full_weight = lax.all_gather(gate_weight, "seq", axis=0, tiled=True)
    gate_sum = jnp.dot(tokens, full_weight, preferred_element_type=jnp.float32)
    gate = gate_sum.astype(jnp.bfloat16).reshape(local_blocks, block_size, channels)
    first_cols = to_columns(first)
    second_cols = jnp.einsum(
        "bia,abc->ibc", right_blocks, first_cols, preferred_element_type=jnp.float32
    ).astype(jnp.bfloat16)
    second = to_rows(second_cols)
    gate_f = gate.astype(jnp.float32)
    factor = jax.nn.silu(gate_f)
    second_f = second.astype(jnp.float32)
    upstream_f = upstream.astype(jnp.float32)
    output = (second_f * factor).astype(jnp.bfloat16)
    second_grad = (upstream_f * factor).astype(jnp.bfloat16)
    gate_delta = (upstream_f * second_f * silu_slope(gate_f)).astype(jnp.bfloat16)
    grad_cols = to_columns(second_grad)
    first_grad_cols = jnp.einsum(
        "bia,ibc->abc", right_blocks, grad_cols, preferred_element_type=jnp.float32
    ).astype(jnp.bfloat16)
    scale_w = channels ** (-0.5)
    right_grad = (
        jnp.einsum("ibc,abc->bia", grad_cols, first_cols, preferred_element_type=jnp.float32)
        * scale_w
    ).astype(jnp.bfloat16)
    first_grad = to_rows(first_grad_cols)
    left_grad = (
        jnp.einsum("ajc,abc->ajb", first_grad, token_grid, preferred_element_type=jnp.float32)
        * scale_w
    ).astype(jnp.bfloat16)
    mixer_part = jnp.einsum(
        "ajb,ajc->abc", left_blocks, first_grad, preferred_element_type=jnp.float32
    ).reshape(tok_rows, channels)
    delta_flat = gate_delta.reshape(tok_rows, channels)
    gate_part = jnp.einsum("tc,kc->tk", delta_flat, full_weight, preferred_element_type=jnp.float32)
    input_grad = (mixer_part + gate_part).astype(jnp.bfloat16)
    weight_term = jnp.einsum("tk,tc->kc", tokens, delta_flat, preferred_element_type=jnp.float32)
    gate_grad = lax.psum_scatter(weight_term, "seq", scatter_dimension=0, tiled=True)
    gate_grad = gate_grad * (tok_rows * seq_count) ** (-0.5)
    return (output.reshape(tok_rows, channels), input_grad, gate_grad, left_grad, right_grad)


F32 = jnp.float32
BF16 = jnp.bfloat16
ROWS = 16
PLANE = 4


def mixer_kernel(
    n, tok_hbm, cot_hbm, wsh, left_hbm, right_hbm,
    tok, left, out, part, fr, lgrad, ggrad, rgrad,
    right, cot, wf, first_s, sg_s, fc, gc, sc, fgc, sr, gate, delta, wt, half, quarter, pair, tail, mix,
    ssem, rsem, ws_sem, wr_sem, gs_sem, gr_sem, lsem, step_sem,
):
    me = lax.axis_index("seq")
    zi, qi = me // PLANE, me % PLANE
    chunks = fc.shape[0]
    blocks, width = tok.shape[0], tok.shape[2]
    nz = n // PLANE
    deep = fc.shape[1] * ROWS
    tile = 256
    per = tile // ROWS
    row_tiles = tok.shape[1] // tile
    owners = per // chunks

    loads = [
        pltpu.make_async_copy(left_hbm, left, lsem.at[0]),
        pltpu.make_async_copy(tok_hbm, tok, lsem.at[1]),
        pltpu.make_async_copy(wsh, wf.at[zi, qi], lsem.at[2]),
        pltpu.make_async_copy(cot_hbm, cot, lsem.at[3]),
        pltpu.make_async_copy(right_hbm, right, lsem.at[4]),
    ]

    gi = lax.axis_index("groups")
    yi, ci = qi // 2, qi % 2
    middle = ((zi + 1) // 2) % 2
    adjacent = 5 + 2 * middle
    facing = nz - 1 - zi

    def tell(sem):
        def signal(dev):
            pl.semaphore_signal(sem, inc=1, device_id={"seq": dev}, device_id_type=pl.DeviceIdType.MESH)

        signal(me + 1 - 2 * ci)
        for c in range(2):
            signal(zi * PLANE + (1 - yi) * 2 + c)
            pl.when(zi > 0)(functools.partial(signal, (zi - 1) * PLANE + yi * 2 + c))
            pl.when(zi < nz - 1)(functools.partial(signal, (zi + 1) * PLANE + yi * 2 + c))

    barrier = pltpu.get_barrier_semaphore()
    pl.semaphore_signal(barrier, inc=1, device_id={"groups": 1 - gi}, device_id_type=pl.DeviceIdType.MESH)
    tell(barrier)
    for load in loads:
        load.start()
    pl.semaphore_wait(barrier, adjacent + 1)

    def remote(src, dst, ss, rs, dev):
        return pltpu.make_async_remote_copy(
            src_ref=src, dst_ref=dst, send_sem=ss, recv_sem=rs,
            device_id={"seq": dev}, device_id_type=pl.DeviceIdType.MESH,
        )

    def to_cols(ph, k, src, dst, s):
        t = (s * 7) % n
        peer = (me + t) % n
        return remote(
            src.at[:, peer * chunks + k], dst.at[k, pl.ds(me * blocks, blocks)],
            ssem.at[ph, k, t], rsem.at[ph, k, t], peer,
        )

    def to_rows_(ph, k, src, dst, s):
        t = s % n
        peer = (me + t) % n
        return remote(
            src.at[k, pl.ds(peer * blocks, blocks)], dst.at[:, k, me],
            ssem.at[ph, k, t], rsem.at[ph, k, t], peer,
        )

    def each(make, action):
        def step(s, carry):
            copy = make(s)
            if action == "start":
                copy.start()
            elif action == "recv":
                copy.wait_recv()
            else:
                copy.wait_send()
            return carry

        lax.fori_loop(1, n, step, 0)

    across = (zi + nz // 2) % nz
    beside = zi + 1 - 2 * (zi % 2)
    own_first = (ci + gi + 1) % 2
    carried = facing * own_first + across * (1 - own_first)
    other_half = pl.ds((1 - zi // 2) * 2, 2)

    w_near = remote(wsh, wf.at[zi, qi], ws_sem.at[0, 1], wr_sem.at[0, 1], beside * PLANE + qi)
    w_own = remote(wsh, wf.at[zi, qi], ws_sem.at[0, 0], wr_sem.at[0, 0], facing * PLANE + qi)
    w_next = remote(wf.at[beside, qi], wf.at[beside, qi], ws_sem.at[0, 0], wr_sem.at[0, 0], facing * PLANE + qi)
    w_got = remote(wf.at[carried, qi], wf.at[carried, qi], ws_sem.at[0, 0], wr_sem.at[0, 0], facing * PLANE + qi)
    w_group = pltpu.make_async_remote_copy(
        src_ref=wf.at[carried, qi], dst_ref=wf.at[carried, qi], send_sem=ws_sem.at[0, 3], recv_sem=wr_sem.at[0, 3],
        device_id={"groups": 1 - gi}, device_id_type=pl.DeviceIdType.MESH,
    )
    w_pass = remote(
        wf.at[other_half, qi], wf.at[other_half, qi], ws_sem.at[0, 2], wr_sem.at[0, 2], beside * PLANE + qi
    )

    mate = me + 1 - 2 * ci
    over = (1 - yi) * 2 + ci
    w_y = remote(wf.at[:, qi], wf.at[:, qi], ws_sem.at[1, 0], wr_sem.at[1, 0], zi * PLANE + over)
    w_core = [
        remote(wf.at[:, q], wf.at[:, q], ws_sem.at[1, 1 + i], wr_sem.at[1, 1 + i], mate)
        for i, q in enumerate((qi, over))
    ]

    w_near.start()

    @pl.when(middle * own_first == 1)
    def _():
        w_own.start()

    tell(step_sem.at[0])
    loads[0].wait()
    loads[1].wait()

    def first_tile(t, carry):
        a, j = t // row_tiles, t % row_tiles
        side = left[a, pl.ds(j * owners, owners)].reshape(tile, left.shape[4])
        prod = jnp.dot(side, tok[a], preferred_element_type=F32)
        first_s[a, pl.ds(j * per, per)] = prod.astype(BF16).reshape(per, ROWS, width)
        return carry

    first_tiles = blocks * row_tiles
    lax.fori_loop(0, first_tiles // 2, first_tile, 0)
    pl.semaphore_wait(step_sem.at[0], adjacent)
    tell(step_sem.at[1])
    lax.fori_loop(first_tiles // 2, first_tiles, first_tile, 0)

    def first_copy(k, t):
        peer = (me + t) % n
        return remote(
            first_s.at[:, peer * chunks + k], fc.at[k, pl.ds(me * blocks, blocks)],
            ssem.at[0, k, t], rsem.at[0, k, t], peer,
        )

    ahead = facing * PLANE + yi * 2

    @pl.when(middle == 1)
    def _():
        for c in range(2):
            first_copy(0, (ahead + c - me + n) % n).start()

    pl.semaphore_wait(step_sem.at[1], adjacent)
    tell(step_sem.at[2])

    @pl.when(middle == 0)
    def _():
        pl.semaphore_wait(step_sem.at[2], adjacent)


    def send_first(k):
        def step(s, carry):
            t = (s * 7) % n
            peer = (me + t) % n
            done = middle * ((peer // 2 * 2 + n - ahead) % n == 0).astype(jnp.int32) if k == 0 else 0

            @pl.when(done == 0)
            def _():
                first_copy(k, t).start()

            return carry

        lax.fori_loop(1, n, step, 0)
        fc[k, pl.ds(me * blocks, blocks)] = first_s[:, me * chunks + k]

    def send_second_grad(k):
        each(functools.partial(to_cols, 1, k, sg_s, gc), "start")
        gc[k, pl.ds(me * blocks, blocks)] = sg_s[:, me * chunks + k]

    w_near.wait_recv()

    @pl.when(middle * (1 - own_first) == 1)
    def _():
        w_next.start()

    send_first(0)

    @pl.when(middle == 1)
    def _():
        pl.semaphore_wait(step_sem.at[2], adjacent)


    @pl.when(middle == 1)
    def _():
        w_got.wait_recv()
        w_group.start()
        w_group.wait_recv()
        w_pass.start()

    for k in range(1, chunks):
        send_first(k)

    loads[2].wait()

    @pl.when(middle == 1)
    def _():
        w_y.start()
        w_core[0].start()

    spread = (
        lax.broadcasted_iota(jnp.int32, (deep // ROWS, deep), 1) // ROWS
        == lax.broadcasted_iota(jnp.int32, (deep // ROWS, deep), 0)
    ).astype(F32).astype(BF16)
    same = (
        lax.broadcasted_iota(jnp.int32, (deep, deep), 0) % ROWS
        == lax.broadcasted_iota(jnp.int32, (deep, deep), 1) % ROWS
    )
    outer = deep // ROWS
    row = lax.broadcasted_iota(jnp.int32, (deep, deep), 0)
    col = lax.broadcasted_iota(jnp.int32, (deep, deep), 1)
    turn = ((row // ROWS == col % outer) & (row % ROWS == col // outer)).astype(F32).astype(BF16)
    loads[4].wait()
    for k in range(chunks):
        rk = jnp.dot(turn, right[k], preferred_element_type=F32).astype(BF16)
        wide = jnp.dot(rk, spread, preferred_element_type=F32)
        mix[k] = jnp.where(same, wide, 0.0).astype(BF16)

    def mixed(k, src, dst, dims):
        def step(t, carry):
            cols = pl.ds(pl.multiple_of(t * tile, tile), tile)
            x = src[k, :, :, cols].reshape(deep, tile)
            y = lax.dot_general(mix[k], x, (dims, ((), ())), preferred_element_type=F32)
            dst[k, :, :, cols] = y.astype(BF16).reshape(deep // ROWS, ROWS, tile)
            return carry

        lax.fori_loop(0, width // tile, step, 0)

    def second_of(k):
        each(functools.partial(to_cols, 0, k, first_s, fc), "recv")
        mixed(k, fc, sc, ((1,), (0,)))
        each(functools.partial(to_rows_, 2, k, sc, sr), "start")
        sr[:, k, me] = sc[k, pl.ds(me * blocks, blocks)]

    def first_grad_of(k):
        each(functools.partial(to_cols, 1, k, sg_s, gc), "recv")
        mixed(k, gc, fgc, ((0,), (0,)))
        each(functools.partial(to_rows_, 3, k, fgc, fr), "start")
        fr[:, k, me] = fgc[k, pl.ds(me * blocks, blocks)]

    second_of(0)

    @pl.when(middle == 0)
    def _():
        w_pass.wait_recv()
        w_y.start()
        w_core[0].start()

    w_y.wait_recv()
    w_core[1].start()
    for k in range(1, chunks):
        second_of(k)

    for copy in w_core:
        copy.wait_recv()
    loads[3].wait()

    def gate_tile(t, carry):
        a, j = t // row_tiles, t % row_tiles
        rows = pl.ds(j * tile, tile)
        weight = wf[...].reshape(width, width)
        g = jnp.dot(tok[a, rows, :], weight, preferred_element_type=F32).astype(BF16)
        gate[a, rows, :] = g
        gf = g.astype(F32)
        up = cot[a, rows, :].astype(F32) * (gf * jax.nn.sigmoid(gf))
        sg_s[a, pl.ds(j * per, per)] = up.astype(BF16).reshape(per, ROWS, width)
        return carry

    lax.fori_loop(0, blocks * row_tiles, gate_tile, 0)
    for k in range(chunks):
        send_second_grad(k)

    for k in range(chunks):
        each(functools.partial(to_rows_, 2, k, sc, sr), "recv")

    def delta_tile(t, carry):
        a, j = t // row_tiles, t % row_tiles
        rows = pl.ds(j * tile, tile)
        gf = gate[a, rows, :].astype(F32)
        sig = jax.nn.sigmoid(gf)
        sec = jnp.stack([sr[a, k, pl.ds(j * owners, owners)] for k in range(chunks)], axis=1)
        sec = sec.reshape(tile, width).astype(F32)
        up = cot[a, rows, :].astype(F32)
        out[a, rows, :] = (sec * (gf * sig)).astype(BF16)
        delta[a, rows, :] = (up * sec * (sig * (1.0 + gf * (1.0 - sig)))).astype(BF16)
        return carry

    lax.fori_loop(0, blocks * row_tiles, delta_tile, 0)
    def weight_tile(z, carry):
        cols = pl.ds(pl.multiple_of(z * tile, tile), tile)
        tokens_2d = tok[:, :, cols].reshape(blocks * tok.shape[1], tile)
        delta_2d = delta[...].reshape(blocks * tok.shape[1], width)
        prod = lax.dot_general(tokens_2d, delta_2d, (((0,), (0,)), ((), ())), preferred_element_type=F32)
        wt[z] = prod.astype(BF16).reshape(PLANE, tile // PLANE, width)
        return carry

    lax.fori_loop(0, width // tile, weight_tile, 0)

    g_core = [
        remote(wt.at[:, 2 * y + 1 - ci], half.at[y], gs_sem.at[0, y], gr_sem.at[0, y], mate) for y in range(2)
    ]
    g_y = remote(wt.at[:, over], half.at[2], gs_sem.at[0, 2], gr_sem.at[0, 2], zi * PLANE + over)
    g_near = [
        remote(quarter.at[beside], tail.at[0], gs_sem.at[1, 0], gr_sem.at[1, 0], beside * PLANE + qi),
        remote(
            quarter.at[(beside + nz // 2) % nz], tail.at[1], gs_sem.at[1, 1], gr_sem.at[1, 1], beside * PLANE + qi
        ),
    ]
    g_far = remote(pair, tail.at[2], gs_sem.at[1, 2], gr_sem.at[1, 2], across * PLANE + qi)

    for copy in g_core:
        copy.start()
    for copy in g_core:
        copy.wait_recv()

    def chip_tile(z, carry):
        wt[z, over] = (wt[z, over].astype(F32) + half[1 - yi, z].astype(F32)).astype(BF16)
        return carry

    lax.fori_loop(0, nz, chip_tile, 0)
    g_y.start()
    first_grad_of(0)
    g_y.wait_recv()

    def sum_tile(z, carry):
        total = wt[z, qi].astype(F32) + half[yi, z].astype(F32) + half[2, z].astype(F32)
        quarter[z] = total.astype(BF16)
        return carry

    lax.fori_loop(0, nz, sum_tile, 0)
    for copy in g_near:
        copy.start()
    def part_tile(t, carry):
        a, j = t // row_tiles, t % row_tiles
        rows = pl.ds(j * tile, tile)
        weight = wf[...].reshape(width, width)
        part[a, rows, :] = lax.dot_general(
            delta[a, rows, :], weight, (((1,), (1,)), ((), ())), preferred_element_type=F32
        )
        return carry

    lax.fori_loop(0, blocks * row_tiles, part_tile, 0)

    for copy in g_near:
        copy.wait_recv()
    pair[...] = (quarter[across].astype(F32) + tail[1].astype(F32)).astype(BF16)
    g_far.start()
    for k in range(1, chunks):
        first_grad_of(k)

    scale_w = width ** (-0.5)
    for k in range(chunks):
        pairs = lax.dot_general(
            gc[k].reshape(deep, width), fc[k].reshape(deep, width),
            (((1,), (1,)), ((), ())), preferred_element_type=F32,
        )
        kept = jnp.where(same, pairs * scale_w, 0.0).astype(BF16)
        picked = lax.dot_general(
            kept, spread, (((1,), (1,)), ((), ())), preferred_element_type=F32
        ).astype(BF16)
        rgrad[k] = lax.dot_general(
            turn, picked, (((0,), (0,)), ((), ())), preferred_element_type=F32
        ).astype(BF16)

    for k in range(chunks):
        each(functools.partial(to_cols, 0, k, first_s, fc), "send")
        each(functools.partial(to_rows_, 2, k, sc, sr), "send")
        each(functools.partial(to_cols, 1, k, sg_s, gc), "send")
    for copy in (w_near, w_y, *w_core, *g_core, g_y, *g_near):
        copy.wait_send()

    @pl.when(middle == 1)
    def _():
        for copy in (w_got, w_group, w_pass):
            copy.wait_send()

    for k in range(chunks - 1):
        each(functools.partial(to_rows_, 3, k, fgc, fr), "recv")

        def near_tile(t, carry):
            a, j = t // row_tiles, t % row_tiles
            rows = pl.ds(pl.multiple_of(j * tile, tile), tile)
            part[a, rows, :] += mixer_of(a, k, rows, left, fr)
            lgrad[a, k, :, :, rows] = left_grad_of(a, k, rows, tok, fr)
            return carry

        lax.fori_loop(0, blocks * row_tiles, near_tile, 0)
        each(functools.partial(to_rows_, 3, k, fgc, fr), "send")

    g_far.wait_recv()
    total = quarter[zi].astype(F32) + tail[0].astype(F32) + tail[2].astype(F32)
    ggrad[...] = total * (blocks * tok.shape[1] * n) ** (-0.5)
    g_far.wait_send()
    for k in range(chunks - 1, chunks):
        each(functools.partial(to_rows_, 3, k, fgc, fr), "send")
        each(functools.partial(to_rows_, 3, k, fgc, fr), "recv")


def mixer_of(a, k, rows, left, fr):
    high = fr.shape[2] * ROWS
    side = left[a, :, k, :, rows].reshape(high, rows.size)
    grad = fr[a, k].reshape(high, fr.shape[4])
    return lax.dot_general(side, grad, (((0,), (0,)), ((), ())), preferred_element_type=F32)


def left_grad_of(a, k, rows, tok, fr):
    high, width = fr.shape[2] * ROWS, fr.shape[4]
    grad = fr[a, k].reshape(high, width)
    lg = lax.dot_general(grad, tok[a, rows, :], (((1,), (1,)), ((), ())), preferred_element_type=F32)
    return (lg * width ** (-0.5)).astype(BF16).reshape(fr.shape[2], ROWS, rows.size)


def last_kernel(
    tok, left, out_in, part, fr, lgrad_in, ggrad_in, rgrad_in,
    out, igrad, lgrad, ggrad, rgrad,
    ig, lg, sem, ig_sem, lg_sem,
):
    blocks, chunks = fr.shape[0], fr.shape[1]
    tile = 256
    last = chunks - 1
    copies = [
        pltpu.make_async_copy(out_in, out, sem.at[0]),
        pltpu.make_async_copy(ggrad_in, ggrad, sem.at[1]),
        pltpu.make_async_copy(rgrad_in, rgrad, sem.at[2]),
    ]
    for k in range(last):
        copies.append(pltpu.make_async_copy(lgrad_in.at[:, k], lgrad.at[:, :, k], sem.at[3 + k]))
    for copy in copies:
        copy.start()
    for a in range(blocks):
        for j in range(tok.shape[1] // tile):
            rows = pl.ds(j * tile, tile)
            lg[a, :, :, rows] = left_grad_of(a, last, rows, tok, fr)
            if j == tok.shape[1] // tile - 1:
                copy = pltpu.make_async_copy(lg.at[a], lgrad.at[a, :, last], lg_sem.at[a])
                copy.start()
                copies.append(copy)
            ig[a, rows, :] = (part[a, rows, :] + mixer_of(a, last, rows, left, fr)).astype(BF16)
            copy = pltpu.make_async_copy(ig.at[a, rows], igrad.at[a, rows], ig_sem.at[a, j])
            copy.start()
            copies.append(copy)
    for copy in copies:
        copy.wait()


def fused_body(n, tokens, cotangent, gate_weight, left_blocks, right_blocks):
    blocks, inner = left_blocks.shape[0], left_blocks.shape[1]
    own, outer = right_blocks.shape[0], right_blocks.shape[1]
    width = tokens.shape[1]
    chunks = own // ROWS
    groups = inner // ROWS
    deep = outer * ROWS
    nz = n // PLANE
    shard = width // n
    rows = (blocks, inner, width)
    split = (blocks, n, chunks, ROWS, inner)
    near = (blocks, chunks - 1, n, ROWS, inner)
    by_row = pltpu.VMEM((blocks, groups, ROWS, width), BF16)
    by_owner = (blocks, chunks, n, ROWS, width)
    by_col = pltpu.VMEM((chunks, outer, ROWS, width), BF16)
    vmem = pl.BlockSpec(memory_space=pltpu.VMEM)
    hbm = pl.BlockSpec(memory_space=pltpu.HBM)
    args = (
        tokens.reshape(rows), cotangent.reshape(rows), gate_weight, left_blocks.reshape(split),
        right_blocks.reshape(chunks, deep, outer),
    )
    kept = pl.pallas_call(
        functools.partial(mixer_kernel, n),
        out_shape=(
            pltpu.VMEM(rows, BF16),
            pltpu.VMEM(split, BF16),
            pltpu.VMEM(rows, BF16),
            pltpu.VMEM(rows, F32),
            pltpu.VMEM(by_owner, BF16),
            pltpu.VMEM(near, BF16),
            pltpu.VMEM((shard, width), F32),
            pltpu.VMEM((chunks, deep, outer), BF16),
        ),
        in_specs=[hbm] * 5,
        out_specs=[vmem] * 8,
        scratch_shapes=[
            pltpu.VMEM((chunks, deep, outer), BF16),
            pltpu.VMEM(rows, BF16),
            pltpu.VMEM((nz, PLANE, shard, width), BF16),
            by_row, by_row, by_col, by_col, by_col, by_col, pltpu.VMEM(by_owner, BF16),
            pltpu.VMEM(rows, BF16),
            pltpu.VMEM(rows, BF16),
            pltpu.VMEM((nz, PLANE, shard, width), BF16),
            pltpu.VMEM((PLANE - 1, nz, shard, width), BF16),
            pltpu.VMEM((nz, shard, width), BF16),
            pltpu.VMEM((shard, width), BF16),
            pltpu.VMEM((3, shard, width), BF16),
            pltpu.VMEM((chunks, deep, deep), BF16),
            pltpu.SemaphoreType.DMA((4, chunks, n)),
            pltpu.SemaphoreType.DMA((4, chunks, n)),
            pltpu.SemaphoreType.DMA((2, PLANE)),
            pltpu.SemaphoreType.DMA((2, PLANE)),
            pltpu.SemaphoreType.DMA((2, PLANE)),
            pltpu.SemaphoreType.DMA((2, PLANE)),
            pltpu.SemaphoreType.DMA((5,)),
            pltpu.SemaphoreType.REGULAR((3,)),
        ],
        compiler_params=pltpu.CompilerParams(
            collective_id=0, has_side_effects=True, vmem_limit_bytes=36 * 2**20
        ),
    )(*[pltpu.with_memory_space_constraint(x, pltpu.HBM) for x in args])
    out, igrad, lgrad, ggrad, rgrad = pl.pallas_call(
        last_kernel,
        out_shape=(
            jax.ShapeDtypeStruct(rows, BF16),
            jax.ShapeDtypeStruct(rows, BF16),
            jax.ShapeDtypeStruct(split, BF16),
            jax.ShapeDtypeStruct((shard, width), F32),
            jax.ShapeDtypeStruct((chunks, deep, outer), BF16),
        ),
        in_specs=[vmem] * 8,
        out_specs=[hbm] * 5,
        scratch_shapes=[
            pltpu.VMEM(rows, BF16),
            pltpu.VMEM((blocks, n, ROWS, inner), BF16),
            pltpu.SemaphoreType.DMA((2 + chunks,)),
            pltpu.SemaphoreType.DMA((blocks, inner // 256)),
            pltpu.SemaphoreType.DMA((blocks,)),
        ],
        compiler_params=pltpu.CompilerParams(vmem_limit_bytes=12 * 2**20),
    )(*[pltpu.with_memory_space_constraint(x, pltpu.VMEM) for x in kept])
    return (
        out.reshape(tokens.shape), igrad.reshape(tokens.shape), ggrad, lgrad.reshape(left_blocks.shape),
        rgrad.reshape(own, outer, outer),
    )


def chosen_body(tokens, cotangent, gate_weight, left_blocks, right_blocks):
    n = lax.axis_size("seq")
    own, width, inner = right_blocks.shape[0], tokens.shape[1], left_blocks.shape[1]
    if lax.axis_size("groups") == 2 and n == PLANE * PLANE and own % ROWS == 0 and width == 256 * PLANE and inner % 256 == 0:
        return fused_body(n, tokens, cotangent, gate_weight, left_blocks, right_blocks)
    return body(tokens, cotangent, gate_weight, left_blocks, right_blocks)


def solution(mesh):
    in_specs = (
        P(("groups", "seq"), None),
        P(("groups", "seq"), None),
        P("seq", None),
        P("seq", None, None),
        P("seq", None, None),
    )
    out_specs = (
        P(("groups", "seq"), None),
        P(("groups", "seq"), None),
        P(("groups", "seq"), None),
        P(("groups", "seq"), None, None),
        P(("groups", "seq"), None, None),
    )
    return jax.shard_map(chosen_body, mesh=mesh, in_specs=in_specs, out_specs=out_specs, check_vma=False)
```

```python
import functools

import jax
import jax.numpy as jnp
from jax import lax
from jax.experimental import pallas as pl
from jax.experimental.pallas import tpu as pltpu
from jax.sharding import PartitionSpec as P


def silu_slope(value):
    sig = jax.nn.sigmoid(value)
    return sig * (1.0 + value * (1.0 - sig))


def to_columns(values):
    return lax.all_to_all(values, "seq", split_axis=1, concat_axis=0, tiled=True)


def to_rows(values):
    return lax.all_to_all(values, "seq", split_axis=0, concat_axis=1, tiled=True)


def body(tokens, cotangent, gate_weight, left_blocks, right_blocks):
    seq_count = lax.axis_size("seq")
    local_blocks = left_blocks.shape[0]
    block_size = left_blocks.shape[1]
    tok_rows = tokens.shape[0]
    channels = tokens.shape[1]
    token_grid = tokens.reshape(local_blocks, block_size, channels)
    upstream = cotangent.reshape(local_blocks, block_size, channels)
    first = jnp.einsum(
        "ajb,abc->ajc", left_blocks, token_grid, preferred_element_type=jnp.float32
    ).astype(jnp.bfloat16)
    full_weight = lax.all_gather(gate_weight, "seq", axis=0, tiled=True)
    gate_sum = jnp.dot(tokens, full_weight, preferred_element_type=jnp.float32)
    gate = gate_sum.astype(jnp.bfloat16).reshape(local_blocks, block_size, channels)
    first_cols = to_columns(first)
    second_cols = jnp.einsum(
        "bia,abc->ibc", right_blocks, first_cols, preferred_element_type=jnp.float32
    ).astype(jnp.bfloat16)
    second = to_rows(second_cols)
    gate_f = gate.astype(jnp.float32)
    factor = jax.nn.silu(gate_f)
    second_f = second.astype(jnp.float32)
    upstream_f = upstream.astype(jnp.float32)
    output = (second_f * factor).astype(jnp.bfloat16)
    second_grad = (upstream_f * factor).astype(jnp.bfloat16)
    gate_delta = (upstream_f * second_f * silu_slope(gate_f)).astype(jnp.bfloat16)
    grad_cols = to_columns(second_grad)
    first_grad_cols = jnp.einsum(
        "bia,ibc->abc", right_blocks, grad_cols, preferred_element_type=jnp.float32
    ).astype(jnp.bfloat16)
    scale_w = channels ** (-0.5)
    right_grad = (
        jnp.einsum("ibc,abc->bia", grad_cols, first_cols, preferred_element_type=jnp.float32)
        * scale_w
    ).astype(jnp.bfloat16)
    first_grad = to_rows(first_grad_cols)
    left_grad = (
        jnp.einsum("ajc,abc->ajb", first_grad, token_grid, preferred_element_type=jnp.float32)
        * scale_w
    ).astype(jnp.bfloat16)
    mixer_part = jnp.einsum(
        "ajb,ajc->abc", left_blocks, first_grad, preferred_element_type=jnp.float32
    ).reshape(tok_rows, channels)
    delta_flat = gate_delta.reshape(tok_rows, channels)
    gate_part = jnp.einsum("tc,kc->tk", delta_flat, full_weight, preferred_element_type=jnp.float32)
    input_grad = (mixer_part + gate_part).astype(jnp.bfloat16)
    weight_term = jnp.einsum("tk,tc->kc", tokens, delta_flat, preferred_element_type=jnp.float32)
    gate_grad = lax.psum_scatter(weight_term, "seq", scatter_dimension=0, tiled=True)
    gate_grad = gate_grad * (tok_rows * seq_count) ** (-0.5)
    return (output.reshape(tok_rows, channels), input_grad, gate_grad, left_grad, right_grad)


F32 = jnp.float32
BF16 = jnp.bfloat16
ROWS = 16
PLANE = 4


def mixer_kernel(
    n, tok_hbm, cot_hbm, wsh, left_hbm, right_hbm,
    tok, left, out, part, fr, lgrad, ggrad, rgrad,
    right, cot, wf, first_s, sg_s, fc, gc, sc, fgc, sr, gate, delta, wt, half, quarter, pair, tail, mix,
    ssem, rsem, ws_sem, wr_sem, gs_sem, gr_sem, lsem, step_sem,
):
    me = lax.axis_index("seq")
    zi, qi = me // PLANE, me % PLANE
    chunks = fc.shape[0]
    blocks, width = tok.shape[0], tok.shape[2]
    nz = n // PLANE
    deep = fc.shape[1] * ROWS
    tile = 256
    per = tile // ROWS
    row_tiles = tok.shape[1] // tile
    owners = per // chunks

    loads = [
        pltpu.make_async_copy(left_hbm, left, lsem.at[0]),
        pltpu.make_async_copy(tok_hbm, tok, lsem.at[1]),
        pltpu.make_async_copy(wsh, wf.at[zi, qi], lsem.at[2]),
        pltpu.make_async_copy(cot_hbm, cot, lsem.at[3]),
        pltpu.make_async_copy(right_hbm, right, lsem.at[4]),
    ]

    gi = lax.axis_index("groups")
    yi, ci = qi // 2, qi % 2
    middle = ((zi + 1) // 2) % 2
    adjacent = 5 + 2 * middle
    facing = nz - 1 - zi

    def tell(sem):
        def signal(dev):
            pl.semaphore_signal(sem, inc=1, device_id={"seq": dev}, device_id_type=pl.DeviceIdType.MESH)

        signal(me + 1 - 2 * ci)
        for c in range(2):
            signal(zi * PLANE + (1 - yi) * 2 + c)
            pl.when(zi > 0)(functools.partial(signal, (zi - 1) * PLANE + yi * 2 + c))
            pl.when(zi < nz - 1)(functools.partial(signal, (zi + 1) * PLANE + yi * 2 + c))

    barrier = pltpu.get_barrier_semaphore()
    pl.semaphore_signal(barrier, inc=1, device_id={"groups": 1 - gi}, device_id_type=pl.DeviceIdType.MESH)
    tell(barrier)
    for load in loads:
        load.start()
    pl.semaphore_wait(barrier, adjacent + 1)

    def remote(src, dst, ss, rs, dev):
        return pltpu.make_async_remote_copy(
            src_ref=src, dst_ref=dst, send_sem=ss, recv_sem=rs,
            device_id={"seq": dev}, device_id_type=pl.DeviceIdType.MESH,
        )

    def to_cols(ph, k, src, dst, s):
        t = (s * 7) % n
        peer = (me + t) % n
        return remote(
            src.at[:, peer * chunks + k], dst.at[k, pl.ds(me * blocks, blocks)],
            ssem.at[ph, k, t], rsem.at[ph, k, t], peer,
        )

    def to_rows_(ph, k, src, dst, s):
        t = s % n
        peer = (me + t) % n
        return remote(
            src.at[k, pl.ds(peer * blocks, blocks)], dst.at[:, k, me],
            ssem.at[ph, k, t], rsem.at[ph, k, t], peer,
        )

    def each(make, action):
        def step(s, carry):
            copy = make(s)
            if action == "start":
                copy.start()
            elif action == "recv":
                copy.wait_recv()
            else:
                copy.wait_send()
            return carry

        lax.fori_loop(1, n, step, 0)

    across = (zi + nz // 2) % nz
    beside = zi + 1 - 2 * (zi % 2)
    own_first = (ci + gi + 1) % 2
    carried = facing * own_first + across * (1 - own_first)
    other_half = pl.ds((1 - zi // 2) * 2, 2)

    w_near = remote(wsh, wf.at[zi, qi], ws_sem.at[0, 1], wr_sem.at[0, 1], beside * PLANE + qi)
    w_own = remote(wsh, wf.at[zi, qi], ws_sem.at[0, 0], wr_sem.at[0, 0], facing * PLANE + qi)
    w_next = remote(wf.at[beside, qi], wf.at[beside, qi], ws_sem.at[0, 0], wr_sem.at[0, 0], facing * PLANE + qi)
    w_got = remote(wf.at[carried, qi], wf.at[carried, qi], ws_sem.at[0, 0], wr_sem.at[0, 0], facing * PLANE + qi)
    w_group = pltpu.make_async_remote_copy(
        src_ref=wf.at[carried, qi], dst_ref=wf.at[carried, qi], send_sem=ws_sem.at[0, 3], recv_sem=wr_sem.at[0, 3],
        device_id={"groups": 1 - gi}, device_id_type=pl.DeviceIdType.MESH,
    )
    w_pass = remote(
        wf.at[other_half, qi], wf.at[other_half, qi], ws_sem.at[0, 2], wr_sem.at[0, 2], beside * PLANE + qi
    )

    mate = me + 1 - 2 * ci
    over = (1 - yi) * 2 + ci
    w_y = remote(wf.at[:, qi], wf.at[:, qi], ws_sem.at[1, 0], wr_sem.at[1, 0], zi * PLANE + over)
    w_core = [
        remote(wf.at[:, q], wf.at[:, q], ws_sem.at[1, 1 + i], wr_sem.at[1, 1 + i], mate)
        for i, q in enumerate((qi, over))
    ]

    w_near.start()

    @pl.when(middle * own_first == 1)
    def _():
        w_own.start()

    tell(step_sem.at[0])
    loads[0].wait()
    loads[1].wait()

    def first_tile(t, carry):
        a, j = t // row_tiles, t % row_tiles
        side = left[a, pl.ds(j * owners, owners)].reshape(tile, left.shape[4])
        prod = jnp.dot(side, tok[a], preferred_element_type=F32)
        first_s[a, pl.ds(j * per, per)] = prod.astype(BF16).reshape(per, ROWS, width)
        return carry

    first_tiles = blocks * row_tiles
    lax.fori_loop(0, first_tiles // 2, first_tile, 0)
    pl.semaphore_wait(step_sem.at[0], adjacent)
    tell(step_sem.at[1])
    lax.fori_loop(first_tiles // 2, first_tiles, first_tile, 0)

    def first_copy(k, t):
        peer = (me + t) % n
        return remote(
            first_s.at[:, peer * chunks + k], fc.at[k, pl.ds(me * blocks, blocks)],
            ssem.at[0, k, t], rsem.at[0, k, t], peer,
        )

    ahead = facing * PLANE + yi * 2

    @pl.when(middle == 1)
    def _():
        for c in range(2):
            first_copy(0, (ahead + c - me + n) % n).start()

    pl.semaphore_wait(step_sem.at[1], adjacent)
    tell(step_sem.at[2])

    @pl.when(middle == 0)
    def _():
        pl.semaphore_wait(step_sem.at[2], adjacent)


    def send_first(k):
        def step(s, carry):
            t = (s * 7) % n
            peer = (me + t) % n
            done = middle * ((peer // 2 * 2 + n - ahead) % n == 0).astype(jnp.int32) if k == 0 else 0

            @pl.when(done == 0)
            def _():
                first_copy(k, t).start()

            return carry

        lax.fori_loop(1, n, step, 0)
        fc[k, pl.ds(me * blocks, blocks)] = first_s[:, me * chunks + k]

    def send_second_grad(k):
        each(functools.partial(to_cols, 1, k, sg_s, gc), "start")
        gc[k, pl.ds(me * blocks, blocks)] = sg_s[:, me * chunks + k]

    w_near.wait_recv()

    @pl.when(middle * (1 - own_first) == 1)
    def _():
        w_next.start()

    send_first(0)

    @pl.when(middle == 1)
    def _():
        pl.semaphore_wait(step_sem.at[2], adjacent)


    @pl.when(middle == 1)
    def _():
        w_got.wait_recv()
        w_group.start()
        w_group.wait_recv()
        w_pass.start()

    for k in range(1, chunks):
        send_first(k)

    loads[2].wait()

    @pl.when(middle == 1)
    def _():
        w_y.start()
        w_core[0].start()

    spread = (
        lax.broadcasted_iota(jnp.int32, (deep // ROWS, deep), 1) // ROWS
        == lax.broadcasted_iota(jnp.int32, (deep // ROWS, deep), 0)
    ).astype(F32).astype(BF16)
    same = (
        lax.broadcasted_iota(jnp.int32, (deep, deep), 0) % ROWS
        == lax.broadcasted_iota(jnp.int32, (deep, deep), 1) % ROWS
    )
    outer = deep // ROWS
    row = lax.broadcasted_iota(jnp.int32, (deep, deep), 0)
    col = lax.broadcasted_iota(jnp.int32, (deep, deep), 1)
    turn = ((row // ROWS == col % outer) & (row % ROWS == col // outer)).astype(F32).astype(BF16)
    loads[4].wait()
    for k in range(chunks):
        rk = jnp.dot(turn, right[k], preferred_element_type=F32).astype(BF16)
        wide = jnp.dot(rk, spread, preferred_element_type=F32)
        mix[k] = jnp.where(same, wide, 0.0).astype(BF16)

    def mixed(k, src, dst, dims):
        def step(t, carry):
            cols = pl.ds(pl.multiple_of(t * tile, tile), tile)
            x = src[k, :, :, cols].reshape(deep, tile)
            y = lax.dot_general(mix[k], x, (dims, ((), ())), preferred_element_type=F32)
            dst[k, :, :, cols] = y.astype(BF16).reshape(deep // ROWS, ROWS, tile)
            return carry

        lax.fori_loop(0, width // tile, step, 0)

    def second_of(k):
        each(functools.partial(to_cols, 0, k, first_s, fc), "recv")
        mixed(k, fc, sc, ((1,), (0,)))
        each(functools.partial(to_rows_, 2, k, sc, sr), "start")
        sr[:, k, me] = sc[k, pl.ds(me * blocks, blocks)]

    def send_first_grad(k, which):
        def step(s, carry):
            peer = (me + s) % n
            late = middle * ((peer // 2 * 2 + n - ahead) % n == 0).astype(jnp.int32)

            @pl.when((which == 2) | (late == which))
            def _():
                to_rows_(3, k, fgc, fr, s).start()

            return carry

        lax.fori_loop(1, n, step, 0)

    def first_grad_of(k):
        each(functools.partial(to_cols, 1, k, sg_s, gc), "recv")
        mixed(k, gc, fgc, ((0,), (0,)))
        send_first_grad(k, 0 if k == chunks - 1 else 2)
        fr[:, k, me] = fgc[k, pl.ds(me * blocks, blocks)]

    second_of(0)

    @pl.when(middle == 0)
    def _():
        w_pass.wait_recv()
        w_y.start()
        w_core[0].start()

    w_y.wait_recv()
    w_core[1].start()
    for k in range(1, chunks):
        second_of(k)

    for copy in w_core:
        copy.wait_recv()
    loads[3].wait()

    def gate_tile(t, carry):
        a, j = t // row_tiles, t % row_tiles
        rows = pl.ds(j * tile, tile)
        weight = wf[...].reshape(width, width)
        g = jnp.dot(tok[a, rows, :], weight, preferred_element_type=F32).astype(BF16)
        gate[a, rows, :] = g
        gf = g.astype(F32)
        up = cot[a, rows, :].astype(F32) * (gf * jax.nn.sigmoid(gf))
        sg_s[a, pl.ds(j * per, per)] = up.astype(BF16).reshape(per, ROWS, width)
        return carry

    lax.fori_loop(0, blocks * row_tiles, gate_tile, 0)
    for k in range(chunks):
        send_second_grad(k)

    for k in range(chunks):
        each(functools.partial(to_rows_, 2, k, sc, sr), "recv")

    def delta_tile(t, carry):
        a, j = t // row_tiles, t % row_tiles
        rows = pl.ds(j * tile, tile)
        gf = gate[a, rows, :].astype(F32)
        sig = jax.nn.sigmoid(gf)
        sec = jnp.stack([sr[a, k, pl.ds(j * owners, owners)] for k in range(chunks)], axis=1)
        sec = sec.reshape(tile, width).astype(F32)
        up = cot[a, rows, :].astype(F32)
        out[a, rows, :] = (sec * (gf * sig)).astype(BF16)
        delta[a, rows, :] = (up * sec * (sig * (1.0 + gf * (1.0 - sig)))).astype(BF16)
        return carry

    lax.fori_loop(0, blocks * row_tiles, delta_tile, 0)
    def weight_tile(z, carry):
        cols = pl.ds(pl.multiple_of(z * tile, tile), tile)
        tokens_2d = tok[:, :, cols].reshape(blocks * tok.shape[1], tile)
        delta_2d = delta[...].reshape(blocks * tok.shape[1], width)
        prod = lax.dot_general(tokens_2d, delta_2d, (((0,), (0,)), ((), ())), preferred_element_type=F32)
        wt[z] = prod.astype(BF16).reshape(PLANE, tile // PLANE, width)
        return carry

    lax.fori_loop(0, width // tile, weight_tile, 0)

    g_core = [
        remote(wt.at[:, 2 * y + 1 - ci], half.at[y], gs_sem.at[0, y], gr_sem.at[0, y], mate) for y in range(2)
    ]
    g_y = remote(wt.at[:, over], half.at[2], gs_sem.at[0, 2], gr_sem.at[0, 2], zi * PLANE + over)
    g_near = [
        remote(quarter.at[beside], tail.at[0], gs_sem.at[1, 0], gr_sem.at[1, 0], beside * PLANE + qi),
        remote(
            quarter.at[(beside + nz // 2) % nz], tail.at[1], gs_sem.at[1, 1], gr_sem.at[1, 1], beside * PLANE + qi
        ),
    ]
    g_far = remote(pair, tail.at[2], gs_sem.at[1, 2], gr_sem.at[1, 2], across * PLANE + qi)

    for copy in g_core:
        copy.start()
    for copy in g_core:
        copy.wait_recv()

    def chip_tile(z, carry):
        wt[z, over] = (wt[z, over].astype(F32) + half[1 - yi, z].astype(F32)).astype(BF16)
        return carry

    lax.fori_loop(0, nz, chip_tile, 0)
    g_y.start()
    first_grad_of(0)
    g_y.wait_recv()

    def sum_tile(z, carry):
        total = wt[z, qi].astype(F32) + half[yi, z].astype(F32) + half[2, z].astype(F32)
        quarter[z] = total.astype(BF16)
        return carry

    lax.fori_loop(0, nz, sum_tile, 0)
    for copy in g_near:
        copy.start()
    def part_tile(t, carry):
        a, j = t // row_tiles, t % row_tiles
        rows = pl.ds(j * tile, tile)
        weight = wf[...].reshape(width, width)
        part[a, rows, :] = lax.dot_general(
            delta[a, rows, :], weight, (((1,), (1,)), ((), ())), preferred_element_type=F32
        )
        return carry

    lax.fori_loop(0, blocks * row_tiles, part_tile, 0)

    for copy in g_near:
        copy.wait_recv()
    pair[...] = (quarter[across].astype(F32) + tail[1].astype(F32)).astype(BF16)
    g_far.start()
    for k in range(1, chunks):
        first_grad_of(k)

    scale_w = width ** (-0.5)
    for k in range(chunks):
        pairs = lax.dot_general(
            gc[k].reshape(deep, width), fc[k].reshape(deep, width),
            (((1,), (1,)), ((), ())), preferred_element_type=F32,
        )
        kept = jnp.where(same, pairs * scale_w, 0.0).astype(BF16)
        picked = lax.dot_general(
            kept, spread, (((1,), (1,)), ((), ())), preferred_element_type=F32
        ).astype(BF16)
        rgrad[k] = lax.dot_general(
            turn, picked, (((0,), (0,)), ((), ())), preferred_element_type=F32
        ).astype(BF16)

    for k in range(chunks):
        each(functools.partial(to_cols, 0, k, first_s, fc), "send")
        each(functools.partial(to_rows_, 2, k, sc, sr), "send")
        each(functools.partial(to_cols, 1, k, sg_s, gc), "send")
    for copy in (w_near, w_y, *w_core, *g_core, g_y, *g_near):
        copy.wait_send()

    @pl.when(middle == 1)
    def _():
        for copy in (w_got, w_group, w_pass):
            copy.wait_send()

    send_first_grad(chunks - 1, 1)
    for k in range(chunks - 1):
        each(functools.partial(to_rows_, 3, k, fgc, fr), "recv")

        def near_tile(t, carry):
            a, j = t // row_tiles, t % row_tiles
            rows = pl.ds(pl.multiple_of(j * tile, tile), tile)
            part[a, rows, :] += mixer_of(a, k, rows, left, fr)
            lgrad[a, k, :, :, rows] = left_grad_of(a, k, rows, tok, fr)
            return carry

        lax.fori_loop(0, blocks * row_tiles, near_tile, 0)
        each(functools.partial(to_rows_, 3, k, fgc, fr), "send")

    g_far.wait_recv()
    total = quarter[zi].astype(F32) + tail[0].astype(F32) + tail[2].astype(F32)
    ggrad[...] = total * (blocks * tok.shape[1] * n) ** (-0.5)
    g_far.wait_send()
    for k in range(chunks - 1, chunks):
        each(functools.partial(to_rows_, 3, k, fgc, fr), "send")
        each(functools.partial(to_rows_, 3, k, fgc, fr), "recv")


def mixer_of(a, k, rows, left, fr):
    high = fr.shape[2] * ROWS
    side = left[a, :, k, :, rows].reshape(high, rows.size)
    grad = fr[a, k].reshape(high, fr.shape[4])
    return lax.dot_general(side, grad, (((0,), (0,)), ((), ())), preferred_element_type=F32)


def left_grad_of(a, k, rows, tok, fr):
    high, width = fr.shape[2] * ROWS, fr.shape[4]
    grad = fr[a, k].reshape(high, width)
    lg = lax.dot_general(grad, tok[a, rows, :], (((1,), (1,)), ((), ())), preferred_element_type=F32)
    return (lg * width ** (-0.5)).astype(BF16).reshape(fr.shape[2], ROWS, rows.size)


def last_kernel(
    tok, left, out_in, part, fr, lgrad_in, ggrad_in, rgrad_in,
    out, igrad, lgrad, ggrad, rgrad,
    ig, lg, sem, ig_sem, lg_sem,
):
    blocks, chunks = fr.shape[0], fr.shape[1]
    tile = 256
    last = chunks - 1
    copies = [
        pltpu.make_async_copy(out_in, out, sem.at[0]),
        pltpu.make_async_copy(ggrad_in, ggrad, sem.at[1]),
        pltpu.make_async_copy(rgrad_in, rgrad, sem.at[2]),
    ]
    for k in range(last):
        copies.append(pltpu.make_async_copy(lgrad_in.at[:, k], lgrad.at[:, :, k], sem.at[3 + k]))
    for copy in copies:
        copy.start()
    for a in range(blocks):
        for j in range(tok.shape[1] // tile):
            rows = pl.ds(j * tile, tile)
            lg[a, :, :, rows] = left_grad_of(a, last, rows, tok, fr)
            if j == tok.shape[1] // tile - 1:
                copy = pltpu.make_async_copy(lg.at[a], lgrad.at[a, :, last], lg_sem.at[a])
                copy.start()
                copies.append(copy)
            ig[a, rows, :] = (part[a, rows, :] + mixer_of(a, last, rows, left, fr)).astype(BF16)
            copy = pltpu.make_async_copy(ig.at[a, rows], igrad.at[a, rows], ig_sem.at[a, j])
            copy.start()
            copies.append(copy)
    for copy in copies:
        copy.wait()


def fused_body(n, tokens, cotangent, gate_weight, left_blocks, right_blocks):
    blocks, inner = left_blocks.shape[0], left_blocks.shape[1]
    own, outer = right_blocks.shape[0], right_blocks.shape[1]
    width = tokens.shape[1]
    chunks = own // ROWS
    groups = inner // ROWS
    deep = outer * ROWS
    nz = n // PLANE
    shard = width // n
    rows = (blocks, inner, width)
    split = (blocks, n, chunks, ROWS, inner)
    near = (blocks, chunks - 1, n, ROWS, inner)
    by_row = pltpu.VMEM((blocks, groups, ROWS, width), BF16)
    by_owner = (blocks, chunks, n, ROWS, width)
    by_col = pltpu.VMEM((chunks, outer, ROWS, width), BF16)
    vmem = pl.BlockSpec(memory_space=pltpu.VMEM)
    hbm = pl.BlockSpec(memory_space=pltpu.HBM)
    args = (
        tokens.reshape(rows), cotangent.reshape(rows), gate_weight, left_blocks.reshape(split),
        right_blocks.reshape(chunks, deep, outer),
    )
    kept = pl.pallas_call(
        functools.partial(mixer_kernel, n),
        out_shape=(
            pltpu.VMEM(rows, BF16),
            pltpu.VMEM(split, BF16),
            pltpu.VMEM(rows, BF16),
            pltpu.VMEM(rows, F32),
            pltpu.VMEM(by_owner, BF16),
            pltpu.VMEM(near, BF16),
            pltpu.VMEM((shard, width), F32),
            pltpu.VMEM((chunks, deep, outer), BF16),
        ),
        in_specs=[hbm] * 5,
        out_specs=[vmem] * 8,
        scratch_shapes=[
            pltpu.VMEM((chunks, deep, outer), BF16),
            pltpu.VMEM(rows, BF16),
            pltpu.VMEM((nz, PLANE, shard, width), BF16),
            by_row, by_row, by_col, by_col, by_col, by_col, pltpu.VMEM(by_owner, BF16),
            pltpu.VMEM(rows, BF16),
            pltpu.VMEM(rows, BF16),
            pltpu.VMEM((nz, PLANE, shard, width), BF16),
            pltpu.VMEM((PLANE - 1, nz, shard, width), BF16),
            pltpu.VMEM((nz, shard, width), BF16),
            pltpu.VMEM((shard, width), BF16),
            pltpu.VMEM((3, shard, width), BF16),
            pltpu.VMEM((chunks, deep, deep), BF16),
            pltpu.SemaphoreType.DMA((4, chunks, n)),
            pltpu.SemaphoreType.DMA((4, chunks, n)),
            pltpu.SemaphoreType.DMA((2, PLANE)),
            pltpu.SemaphoreType.DMA((2, PLANE)),
            pltpu.SemaphoreType.DMA((2, PLANE)),
            pltpu.SemaphoreType.DMA((2, PLANE)),
            pltpu.SemaphoreType.DMA((5,)),
            pltpu.SemaphoreType.REGULAR((3,)),
        ],
        compiler_params=pltpu.CompilerParams(
            collective_id=0, has_side_effects=True, vmem_limit_bytes=36 * 2**20
        ),
    )(*[pltpu.with_memory_space_constraint(x, pltpu.HBM) for x in args])
    out, igrad, lgrad, ggrad, rgrad = pl.pallas_call(
        last_kernel,
        out_shape=(
            jax.ShapeDtypeStruct(rows, BF16),
            jax.ShapeDtypeStruct(rows, BF16),
            jax.ShapeDtypeStruct(split, BF16),
            jax.ShapeDtypeStruct((shard, width), F32),
            jax.ShapeDtypeStruct((chunks, deep, outer), BF16),
        ),
        in_specs=[vmem] * 8,
        out_specs=[hbm] * 5,
        scratch_shapes=[
            pltpu.VMEM(rows, BF16),
            pltpu.VMEM((blocks, n, ROWS, inner), BF16),
            pltpu.SemaphoreType.DMA((2 + chunks,)),
            pltpu.SemaphoreType.DMA((blocks, inner // 256)),
            pltpu.SemaphoreType.DMA((blocks,)),
        ],
        compiler_params=pltpu.CompilerParams(vmem_limit_bytes=12 * 2**20),
    )(*[pltpu.with_memory_space_constraint(x, pltpu.VMEM) for x in kept])
    return (
        out.reshape(tokens.shape), igrad.reshape(tokens.shape), ggrad, lgrad.reshape(left_blocks.shape),
        rgrad.reshape(own, outer, outer),
    )


def chosen_body(tokens, cotangent, gate_weight, left_blocks, right_blocks):
    n = lax.axis_size("seq")
    own, width, inner = right_blocks.shape[0], tokens.shape[1], left_blocks.shape[1]
    if lax.axis_size("groups") == 2 and n == PLANE * PLANE and own % ROWS == 0 and width == 256 * PLANE and inner % 256 == 0:
        return fused_body(n, tokens, cotangent, gate_weight, left_blocks, right_blocks)
    return body(tokens, cotangent, gate_weight, left_blocks, right_blocks)


def solution(mesh):
    in_specs = (
        P(("groups", "seq"), None),
        P(("groups", "seq"), None),
        P("seq", None),
        P("seq", None, None),
        P("seq", None, None),
    )
    out_specs = (
        P(("groups", "seq"), None),
        P(("groups", "seq"), None),
        P(("groups", "seq"), None),
        P(("groups", "seq"), None, None),
        P(("groups", "seq"), None, None),
    )
    return jax.shard_map(chosen_body, mesh=mesh, in_specs=in_specs, out_specs=out_specs, check_vma=False)
```
